128 devices in a mesh: attn: 8 (over z, core), expert: 16 (over x, y).
Axes of the slice: x: 4, y: 4, z: 4, core: 2. Of those that a mesh axis runs over, the one named last changes fastest.
Arguments:
- stream_in: bfloat16 [1024, 4096], P(('attn', 'expert')), may hold values from -48 to 48
- norm_gain: bfloat16 [4096], replicated, may hold values from 0.5 to 1.5
- expert_ids: int32 [1024, 8], P(('attn', 'expert')), may hold values from 0 to 63, as said below
- route_weights: float32 [1024, 8], P(('attn', 'expert')), may hold values from 0.1 to 1
- w_gate: bfloat16 [64, 1536, 4096], P('expert', 'attn'), may hold values from -0.09375 to 0.09375
- w_up: bfloat16 [64, 1536, 4096], P('expert', 'attn'), may hold values from -0.09375 to 0.09375
- w_down: bfloat16 [64, 1536, 4096], P('expert', 'attn'), may hold values from -0.15625 to 0.15625
Outputs:
- expert_mix: float32 [1024, 4096], P(('attn', 'expert'))
The draws below stay inside these ranges and needn't reach their ends.
Inputs may be any that keep to these rules, and one draw needn't show every extreme that they name: `expert_ids`: each row names 8 different experts; the tokens of one device name no expert more than 2 times, and one expert is named exactly 2 times by the tokens of every device.
All inputs are finite; a program needn't handle non-finite values.
Results may differ from the reference program's by a relative error of at most 0.014.
Values may be sent and summed in bfloat16 or wider, within the bound.
A program may use at most 128 MiB of HBM per device.

```python
import math
import jax
import jax.numpy as jnp
from jax import lax

D = 4096
FF = 1536
TOP = 8
ROWS = 8
EXPERTS = 64
TOKENS = 1024
MOST = 2
SLICE = 192
N_ATTN = 8
N_EXPERT = 16


def log_uniform(key, shape, lower, upper):
    return jnp.exp(jax.random.uniform(key, shape, jnp.float32, jnp.log(lower), jnp.log(upper)))


def draw_stream_in(key, part):
    keys = jax.random.split(key, 3)
    column_scale = log_uniform(keys[1], (1, D), 0.3, 3.0)
    base = jnp.clip(jax.random.normal(keys[0], (TOKENS, D), jnp.float32), -4.0, 4.0)
    row_scale = log_uniform(keys[2], (TOKENS, 1), 0.3, 3.0)
    return (base * row_scale * column_scale).astype(jnp.bfloat16)


def random_order(key, blocks, count):
    scores = jax.random.randint(key, (blocks, count), 0, 1 << 20) * count + jnp.arange(count, dtype=jnp.int32)[None, :]
    return jnp.argsort(scores, axis=1).astype(jnp.int32)


def draw_expert_ids(key, part):
    blocks = TOKENS // ROWS
    others_count = EXPERTS - 3
    keys = jax.random.split(key, 8)
    first = jax.random.randint(keys[0], (EXPERTS,), 0, 1 << 20) * EXPERTS + jnp.arange(EXPERTS, dtype=jnp.int32)
    order = jnp.argsort(first).astype(jnp.int32)
    hottest = order[:3]
    others = order[3:]
    listed = others[random_order(keys[1], blocks, others_count)]
    repeats = TOP * ROWS // others_count + 2
    tiled = jnp.tile(listed, (1, repeats))
    rank_one = jnp.argsort(random_order(keys[2], blocks, ROWS), axis=1).astype(jnp.int32)
    rank_two = jnp.argsort(random_order(keys[3], blocks, ROWS), axis=1).astype(jnp.int32)
    rank_three = jnp.argsort(random_order(keys[4], blocks, ROWS), axis=1).astype(jnp.int32)
    count_two = jax.random.randint(keys[5], (blocks, 1), 0, MOST + 1)
    count_three = jax.random.randint(keys[6], (blocks, 1), 0, MOST + 1)
    flags = jnp.stack([(rank_one < MOST).astype(jnp.int32), (rank_two < count_two).astype(jnp.int32), (rank_three < count_three).astype(jnp.int32)], axis=2)
    hot_count = jnp.sum(flags, axis=2)
    length = TOP - hot_count
    begin = jnp.cumsum(length, axis=1) - length
    place = jnp.cumsum(flags, axis=2) - flags
    column = jnp.arange(TOP, dtype=jnp.int32)
    where_listed = jnp.clip(begin[:, :, None] + column[None, None, :] - hot_count[:, :, None], 0, None)
    from_list = jnp.take_along_axis(tiled, where_listed.reshape(blocks, ROWS * TOP), axis=1).reshape(blocks, ROWS, TOP)
    hot_entry = jnp.zeros((blocks, ROWS, TOP), jnp.int32)
    for which in range(3):
        taken = (flags[:, :, which:which + 1] == 1) & (place[:, :, which:which + 1] == column[None, None, :])
        hot_entry = hot_entry + jnp.where(taken, hottest[which], 0)
    chosen = jnp.where(column[None, None, :] < hot_count[:, :, None], hot_entry, from_list)
    rotate = jax.random.randint(keys[7], (blocks, ROWS, 1), 0, TOP)
    chosen = jnp.take_along_axis(chosen, (column[None, None, :] + rotate) % TOP, axis=2)
    return chosen.reshape(TOKENS, TOP).astype(jnp.int32)


def level_of(own_key, shape, pieces, smallest, high):
    gain = 1.0
    for position, shards_of in pieces:
        heights = jax.random.uniform(jax.random.fold_in(jax.random.fold_in(own_key, 6), position), (shards_of,), jnp.float32, smallest / len(pieces), high / len(pieces))
        gain = gain * jnp.repeat(jnp.exp(heights), shape[position] // shards_of).reshape((-1,) + (1,) * (len(shape) - 1 - position))
    return gain


def bell_draw(key, extent, deviation, bound, cuts=(), held_as=jnp.bfloat16):
    result = deviation * jax.random.normal(key, extent, jnp.float32)
    if cuts:
        result = result * level_of(key, extent, cuts, -0.22, 0.18)
    return jnp.clip(result, -bound, bound).astype(held_as)


def setup_inputs(seed: int = 0) -> dict:
    splits = jax.random.split(jax.random.key(seed), 8)
    stream_in = draw_stream_in(jax.random.fold_in(splits[7], 71), 0)
    norm_gain = jnp.clip(jax.random.uniform(splits[1], (D,), jnp.float32, 0.5, 1.5), 0.5, 1.5).astype(jnp.bfloat16)
    expert_ids = draw_expert_ids(jax.random.fold_in(splits[7], 71), 0)
    route_weights = jnp.clip(jnp.exp(math.log(1.0) - 2.3025851 * jax.random.uniform(splits[3], (TOKENS, TOP), jnp.float32) ** level_of(splits[3], (TOKENS, TOP), ((0, 128),), -0.2, 0.2)), 0.1, 1.0)
    w_gate = bell_draw(splits[4], (EXPERTS, FF, D), D ** -0.5, 0.09375, ((0, 16), (1, 8)))
    w_up = bell_draw(splits[5], (EXPERTS, FF, D), D ** -0.5, 0.09375, ((0, 16), (1, 8)))
    w_down = bell_draw(splits[6], (EXPERTS, FF, D), FF ** -0.5, 0.15625, ((0, 16), (1, 8)))
    return dict(stream_in=stream_in, norm_gain=norm_gain, expert_ids=expert_ids, route_weights=route_weights, w_gate=w_gate, w_up=w_up, w_down=w_down)


def reference(stream_in, norm_gain, expert_ids, route_weights, w_gate, w_up, w_down):
    device_count = N_ATTN * N_EXPERT
    stream = stream_in.astype(jnp.float32)
    inverse = lax.rsqrt(lax.optimization_barrier(jnp.mean(stream * stream, axis=-1, keepdims=True)) + 1e-06)
    normed = (stream * inverse * norm_gain.astype(jnp.float32)).astype(jnp.bfloat16)
    blocked_ids = expert_ids.reshape(device_count, ROWS, TOP)
    blocked_weights = route_weights.reshape(device_count, ROWS, TOP)
    blocked_rows = normed.reshape(device_count, ROWS, D).astype(jnp.float32)
    slot_range = jnp.arange(MOST, dtype=jnp.int32)

    def one_expert(totals, inputs):
        gate_matrix, up_matrix, down_matrix, index = inputs
        hit = blocked_ids == index
        named = jnp.any(hit, axis=-1).astype(jnp.int32)
        earlier = jnp.cumsum(named, axis=1) - named
        weight = lax.optimization_barrier(jnp.sum(jnp.where(hit, blocked_weights, jnp.zeros_like(blocked_weights)), axis=-1))
        select = ((named[:, :, None] == 1) & (earlier[:, :, None] == slot_range[None, None, :])).astype(jnp.float32)
        gathered = jnp.einsum('nrm,nrd->nmd', select, blocked_rows, precision=lax.Precision.HIGHEST)
        gathered = gathered.astype(jnp.bfloat16).reshape(device_count * MOST, D)
        gate = jnp.dot(gathered, gate_matrix.T, preferred_element_type=jnp.float32)
        up = jnp.dot(gathered, up_matrix.T, preferred_element_type=jnp.float32)
        act = (jax.nn.silu(gate) * up).astype(jnp.bfloat16)
        parts = jnp.einsum('rsf,sfd->rsd', act.reshape(device_count * MOST, N_ATTN, SLICE).astype(jnp.float32), down_matrix.reshape(N_ATTN, SLICE, D).astype(jnp.float32))
        rounded = lax.optimization_barrier(parts.astype(jnp.bfloat16)).astype(jnp.float32)
        outputs = lax.optimization_barrier(jnp.sum(rounded, axis=1)).reshape(device_count, MOST, D)
        mixer = select * weight[:, :, None]
        added = jnp.einsum('nrm,nmd->nrd', mixer, outputs, precision=lax.Precision.HIGHEST)
        return (totals + added, None)
    initial = jnp.zeros((device_count, ROWS, D), jnp.float32)
    totals, _ = lax.scan(one_expert, initial, (w_gate, w_up, w_down, jnp.arange(EXPERTS, dtype=jnp.int32)))
    return totals.reshape(TOKENS, D)
```

```python
import jax
import jax.numpy as jnp
from jax import lax
from jax.sharding import PartitionSpec as P

AXES = ("attn", "expert")


def local(stream_in, norm_gain, expert_ids, route_weights, w_gate, w_up, w_down):
    held_count, slice_size, feature_count = w_gate.shape
    expert_size = lax.axis_size("expert")
    expert_total = held_count * expert_size
    first = lax.axis_index("expert") * held_count
    stream = stream_in.astype(jnp.float32)
    inverse = lax.rsqrt(jnp.mean(stream * stream, axis=-1, keepdims=True) + 1e-06)
    normed = (stream * inverse * norm_gain.astype(jnp.float32)).astype(jnp.bfloat16)
    hit = expert_ids[:, :, None] == jnp.arange(expert_total, dtype=jnp.int32)[None, None, :]
    weight = jnp.sum(jnp.where(hit, route_weights[:, :, None], 0.0), axis=1)
    weight = jnp.pad(weight, ((0, 0), (0, 128 - expert_total)))
    tokens = lax.all_gather(normed, AXES, axis=0, tiled=True)
    weights = lax.all_gather(weight, AXES, axis=0, tiled=True)
    mine = lax.dynamic_slice_in_dim(weights, first, held_count, axis=1)
    wg = w_gate.reshape(held_count * slice_size, feature_count)
    wu = w_up.reshape(held_count * slice_size, feature_count)
    wd = w_down.reshape(held_count * slice_size, feature_count)
    dims = (((1,), (1,)), ((), ()))
    gate = lax.dot_general(tokens, wg, dims, preferred_element_type=jnp.float32)
    up = lax.dot_general(tokens, wu, dims, preferred_element_type=jnp.float32)
    scale = jnp.repeat(mine, slice_size, axis=1)
    act = (jax.nn.silu(gate) * up * scale).astype(jnp.bfloat16)
    out = jnp.dot(act, wd, preferred_element_type=jnp.float32).astype(jnp.bfloat16)
    mixed = lax.psum_scatter(out, AXES, scatter_dimension=0, tiled=True)
    return mixed.astype(jnp.float32)


def solution(mesh):
    return jax.shard_map(
        local,
        mesh=mesh,
        in_specs=(
            P(("attn", "expert"), None),
            P(),
            P(("attn", "expert"), None),
            P(("attn", "expert"), None),
            P("expert", "attn", None),
            P("expert", "attn", None),
            P("expert", "attn", None),
        ),
        out_specs=P(("attn", "expert"), None),
        check_vma=False,
    )
```

```python
import functools
import jax
import jax.numpy as jnp
from jax import lax
from jax.experimental import pallas as pl
from jax.experimental.pallas import tpu as pltpu
from jax.sharding import PartitionSpec as P

BF = jnp.bfloat16
F32 = jnp.float32
MESH = pl.DeviceIdType.MESH
NT = (((1,), (1,)), ((), ()))

ORDER = ((0, 1, 2), (1, 2, 0), (2, 0, 1))
XW = 4352
HI, LO = 2816, 4224
GSTART, GWIDTH = (0, 1536, 2816), (768, 640, 768)
XK = ((0, 1536), (1536, 1280), (2944, 1280))
WK = ((0, 1536), (1536, 1280), (2816, 1280))
OSTART, OWIDTH, VSTART = (0, 1536, 2816), (768, 640, 640), (0, 768, 1408)
STEPS = (1, -1, 2)


def body(
    x_ref, gain_ref, ids_ref, rw_ref, wg_hbm, wu_hbm, wd_hbm, out_ref,
    X, XB, XS, WG, WU, WD, G, U, A, V, RA, RF, R2, R3, FB, OB, E, N, ss, rs, wsem, *, table,
):
    attn, expert = lax.axis_index("attn"), lax.axis_index("expert")
    m = (expert // 4, expert % 4, attn // 2)
    c = attn % 2

    def device(axis, step):
        n = [m[0], m[1], m[2]]
        n[axis] = (n[axis] + step + 4) % 4
        return (2 * n[2] + c, 4 * n[0] + n[1])

    sibling = (2 * m[2] + 1 - c, expert)

    def coord(axis, step):
        return (m[axis] + step + 4) % 4

    def copy(key, src, dst, dev):
        number = table.setdefault(key, len(table))
        return pltpu.make_async_remote_copy(
            src_ref=src, dst_ref=dst, send_sem=ss.at[number], recv_sem=rs.at[number],
            device_id=dev, device_id_type=MESH,
        )

    def plane_index(axis, q, half=None):
        idx = [slice(None)] * 3
        idx[axis] = q
        if half is not None:
            idx[0 if axis != 0 else 1] = pl.ds(2 * half, 2)
        return tuple(idx)

    def line_index(along, fixed):
        return tuple(slice(None) if a == along else fixed[a] for a in range(3))

    def gcols(p, core):
        return pl.ds(pl.multiple_of(GSTART[p] + core * GWIDTH[p], 128), GWIDTH[p])

    def ocols(p, core):
        return pl.ds(pl.multiple_of(OSTART[p] + core * OWIDTH[p], 128), OWIDTH[p])

    def vcols(p):
        return pl.ds(VSTART[p], OWIDTH[p])

    loads = [
        pltpu.make_async_copy(h, v, wsem.at[i])
        for i, (h, v) in enumerate(((wg_hbm, WG), (wu_hbm, WU), (wd_hbm, WD)))
    ]
    for load in loads:
        load.start()

    barrier = pltpu.get_barrier_semaphore()
    partners = [sibling] + [device(a, s) for a in range(3) for s in STEPS]
    for dev in partners:
        pl.semaphore_signal(barrier, inc=1, device_id=dev, device_id_type=MESH)

    lane = lax.broadcasted_iota(jnp.int32, (8, 128), 1)
    spread = jnp.zeros((8, 128), F32)
    for k in range(8):
        spread = spread + jnp.where(ids_ref[:, k : k + 1] == lane, rw_ref[:, k : k + 1], 0.0)
    high = spread.astype(BF)
    low = (spread - high.astype(F32)).astype(BF)
    XB[:, 0:4096] = x_ref[...]
    XB[:, 4096:4224] = high
    XB[:, 4224:4352] = low
    pl.semaphore_wait(barrier, len(partners))
    swap = copy("swap", XB, XS, sibling)
    swap.start()

    er = lax.broadcasted_iota(jnp.int32, (128, 768), 0)
    ec = lax.broadcasted_iota(jnp.int32, (128, 768), 1)
    held = er - 4 * expert
    E[...] = jnp.where((ec >= held * 192) & (ec < held * 192 + 192), 1.0, 0.0).astype(BF)

    swap.wait()
    mine, other = XB[...].astype(F32), XS[...].astype(F32)
    first = c == 0
    rows = jnp.concatenate([jnp.where(first, mine, other), jnp.where(first, other, mine)], axis=0)
    stream = rows[:, 0:4096]
    inverse = lax.rsqrt(jnp.sum(stream * stream, axis=-1, keepdims=True) * (1.0 / 4096) + 1e-06)
    normed = (stream * inverse * gain_ref[...].astype(F32)).astype(BF)
    N[:, 0:HI] = normed[:, 0:HI]
    N[:, HI : HI + 128] = rows[:, 4096:4224].astype(BF)
    N[:, HI + 128 : LO] = normed[:, HI:4096]
    N[:, LO:XW] = rows[:, 4224:4352].astype(BF)
    for p in range(3):
        X[m[0], m[1], m[2], :, gcols(p, c)] = N[:, gcols(p, c)]

    sends = []

    def start(cp):
        cp.start()
        sends.append(cp)

    def landed(key, ref):
        copy(key, ref, ref, sibling).wait_recv()

    def stage1(p):
        a = ORDER[p][0]
        ref = X.at[m[0], m[1], m[2], :, gcols(p, c)]
        for s in STEPS:
            start(copy(("g1", p, s), ref, ref, device(a, s)))

    def stage2(p):
        a, b, _ = ORDER[p]
        for s in STEPS:
            fixed = list(m)
            fixed[a] = coord(a, -s)
            landed(("g1", p, s), X.at[fixed[0], fixed[1], fixed[2], :, gcols(p, c)])
        ref = X.at[line_index(a, m) + (slice(None), gcols(p, c))]
        for s in STEPS:
            start(copy(("g2", p, s), ref, ref, device(b, s)))

    def xplane(p, q, core, half=None):
        return X.at[plane_index(ORDER[p][2], q, half) + (slice(None), gcols(p, core))]

    def stage3(p):
        a, b, k = ORDER[p]
        for s in STEPS:
            fixed = list(m)
            fixed[b] = coord(b, -s)
            landed(("g2", p, s), X.at[line_index(a, fixed) + (slice(None), gcols(p, c))])
        for n in range(2):
            for s, half in ((1, n), (-1, 1 - n)):
                ref = xplane(p, m[k], c, half)
                start(copy(("g3", p, s, half), ref, ref, device(k, s)))
        ref = xplane(p, m[k], c)
        start(copy(("gs", p, 0), ref, ref, sibling))

    def relay(p):
        k = ORDER[p][2]
        for s, half in ((1, 0), (-1, 1)):
            ref = xplane(p, coord(k, -s), c, half)
            landed(("g3", p, s, half), ref)
            start(copy(("gr", p, s), ref, ref, device(k, s)))

    def share(p):
        k = ORDER[p][2]
        for s, half in ((1, 1), (-1, 0)):
            landed(("g3", p, s, half), xplane(p, coord(k, -s), c, half))
            ref = xplane(p, coord(k, -s), c)
            start(copy(("gs", p, s), ref, ref, sibling))

    def share_far(p):
        k = ORDER[p][2]
        for s, half in ((1, 0), (-1, 1)):
            landed(("gr", p, s), xplane(p, coord(k, 2), c, half))
        ref = xplane(p, coord(k, 2), c)
        start(copy(("gs", p, 2), ref, ref, sibling))

    def unit(p, s):
        k = ORDER[p][2]
        q = coord(k, -s)
        landed(("gs", p, s), xplane(p, q, 1 - c))
        index = plane_index(k, q)
        x0, xn = XK[p]
        w0, wn = WK[p]

        @pl.loop(0, 3)
        def _(n):
            hs = pl.ds(pl.multiple_of(n * 256, 256), 256)
            xs = X[index + (slice(None), slice(x0, x0 + xn))].reshape(256, xn)
            for w, acc in ((WG, G), (WU, U)):
                r = lax.dot_general(xs, w[hs, w0 : w0 + wn], NT, preferred_element_type=F32)
                acc[index + (slice(None), hs)] += r.reshape(4, 4, 16, 256)

    for p in range(3):
        stage1(p)

    @pl.loop(0, 16)
    def _(i):
        G[i // 4, i % 4] = jnp.zeros((4, 16, 768), F32)
        U[i // 4, i % 4] = jnp.zeros((4, 16, 768), F32)

    for p in range(3):
        stage2(p)
    for p in range(3):
        stage3(p)
    loads[0].wait()
    loads[1].wait()
    for p in range(3):
        unit(p, 0)
    for p in range(3):
        relay(p)
    for p in range(3):
        share(p)
    for p in range(3):
        unit(p, 1)
    for p in range(3):
        share_far(p)
    for p in range(3):
        unit(p, -1)
    for p in range(3):
        unit(p, 2)
    loads[2].wait()
    for cp in sends:
        cp.wait_send()
    sends.clear()

    @pl.loop(0, 16)
    def _(i):
        at = (i // 4, i % 4)
        g = G[at].reshape(64, 768)
        u = U[at].reshape(64, 768)
        hi = X[at + (slice(None), slice(None), slice(HI, HI + 128))].reshape(64, 128)
        lo = X[at + (slice(None), slice(None), slice(LO, LO + 128))].reshape(64, 128)
        w = jnp.dot(hi, E[...], preferred_element_type=F32) + jnp.dot(
            lo, E[...], preferred_element_type=F32
        )
        A[at] = (g / (1.0 + jnp.exp(-g)) * u * w).astype(BF).reshape(4, 16, 768)

    def down(p, s):
        k = ORDER[p][2]
        q = coord(k, s)
        index = plane_index(k, q)
        step = (512, 640, 640)[p]

        @pl.loop(0, 2 * OWIDTH[p] // step)
        def _(n):
            cs = pl.ds(pl.multiple_of(OSTART[p] + n * step, 128), step)
            a = A[index].reshape(256, 768)
            r = jnp.dot(a, WD[:, cs], preferred_element_type=F32)
            X[index + (slice(None), cs)] = r.astype(BF).reshape(4, 4, 16, step)

        start(
            copy(
                ("rs", p, s),
                X.at[index + (slice(None), ocols(p, 1 - c))],
                V.at[index + (slice(None), vcols(p))],
                sibling,
            )
        )

    def row_index(axis, q, i):
        rest = [a for a in range(3) if a != axis]
        idx = [None] * 3
        idx[axis] = q
        idx[rest[0]] = i
        idx[rest[1]] = slice(None)
        return tuple(idx)

    def paired(p, s):
        k = ORDER[p][2]
        q = coord(k, s)
        landed(("rs", p, s), V.at[plane_index(k, q) + (slice(None), vcols(p))])

        @pl.loop(0, 4)
        def _(i):
            at = row_index(k, q, i)
            o = at + (slice(None), ocols(p, c))
            X[o] = (X[o].astype(F32) + V[at + (slice(None), vcols(p))].astype(F32)).astype(BF)

    def oplane(p, q, half=None):
        return X.at[plane_index(ORDER[p][2], q, half) + (slice(None), ocols(p, c))]

    def send_far(p):
        k = ORDER[p][2]
        for s, half in ((1, 0), (-1, 1)):
            start(
                copy(
                    ("ra", p, s), oplane(p, coord(k, 2), half),
                    RA.at[pl.ds(2 * half, 2), :, :, vcols(p)], device(k, s),
                )
            )

    def send_half(p, s, half):
        k = ORDER[p][2]
        slot = 0 if s == 1 else 1
        start(
            copy(
                ("rf", p, s, half), oplane(p, coord(k, s), half),
                RF.at[slot, pl.ds(2 * half, 2), :, :, vcols(p)], device(k, s),
            )
        )

    def relay_back(p):
        k = ORDER[p][2]
        for s, half in ((1, 0), (-1, 1)):
            landed(("ra", p, s), RA.at[pl.ds(2 * half, 2), :, :, vcols(p)])
            q = coord(k, s)

            @pl.loop(2 * half, 2 * half + 2)
            def _(i):
                o = row_index(k, q, i) + (slice(None), ocols(p, c))
                X[o] = (X[o].astype(F32) + RA[i, :, :, vcols(p)].astype(F32)).astype(BF)

            send_half(p, s, half)

    def gather_planes(p):
        a, b, k = ORDER[p]
        for s in (1, -1):
            for half in range(2):
                slot = 0 if s == 1 else 1
                landed(("rf", p, s, half), RF.at[slot, pl.ds(2 * half, 2), :, :, vcols(p)])

        @pl.loop(0, 4)
        def _(i):
            o = row_index(k, m[k], i) + (slice(None), ocols(p, c))
            X[o] = (
                X[o].astype(F32)
                + RF[0, i, :, :, vcols(p)].astype(F32)
                + RF[1, i, :, :, vcols(p)].astype(F32)
            ).astype(BF)

        for n, s in enumerate(STEPS):
            fixed = list(m)
            fixed[b] = coord(b, s)
            start(
                copy(
                    ("r2", p, s), X.at[line_index(a, fixed) + (slice(None), ocols(p, c))],
                    R2.at[n, :, :, vcols(p)], device(b, s),
                )
            )

    def gather_lines(p):
        a = ORDER[p][0]
        for n, s in enumerate(STEPS):
            landed(("r2", p, s), R2.at[n, :, :, vcols(p)])
        o = line_index(a, m) + (slice(None), ocols(p, c))
        total = X[o].astype(F32)
        for n in range(3):
            total = total + R2[n, :, :, vcols(p)].astype(F32)
        X[o] = total.astype(BF)
        for n, s in enumerate(STEPS):
            fixed = list(m)
            fixed[a] = coord(a, s)
            start(
                copy(
                    ("r3", p, s), X.at[fixed[0], fixed[1], fixed[2], :, ocols(p, c)],
                    R3.at[n, :, vcols(p)], device(a, s),
                )
            )

    def gather_blocks(p):
        for n, s in enumerate(STEPS):
            landed(("r3", p, s), R3.at[n, :, vcols(p)])
        total = X[m[0], m[1], m[2], :, ocols(p, c)].astype(F32)
        for n in range(3):
            total = total + R3[n, :, vcols(p)].astype(F32)
        FB[:, vcols(p)] = total
        start(
            copy(
                ("r4", p), FB.at[pl.ds(pl.multiple_of(8 * (1 - c), 8), 8), vcols(p)],
                OB.at[:, ocols(p, c)], sibling,
            )
        )
        OB[:, ocols(p, c)] = FB[pl.ds(pl.multiple_of(8 * c, 8), 8), vcols(p)]

    for p in range(3):
        down(p, 2)
    for p in range(3):
        down(p, 1)
        paired(p, 2)
        send_far(p)
    for p in range(3):
        down(p, -1)
        paired(p, 1)
        send_half(p, 1, 1)
    for p in range(3):
        down(p, 0)
        paired(p, -1)
        send_half(p, -1, 0)
    for p in range(3):
        relay_back(p)
    for p in range(3):
        paired(p, 0)
    for p in range(3):
        gather_planes(p)
    for p in range(3):
        gather_lines(p)
    for p in range(3):
        gather_blocks(p)
    for p in range(3):
        landed(("r4", p), OB.at[:, ocols(p, 1 - c)])
    out_ref[...] = OB[...]
    for cp in sends:
        cp.wait_send()


def local(stream_in, norm_gain, expert_ids, route_weights, w_gate, w_up, w_down):
    hidden, features = w_gate.shape[0] * w_gate.shape[1], w_gate.shape[2]
    vmem = pl.BlockSpec(memory_space=pltpu.VMEM)
    hbm = pl.BlockSpec(memory_space=pl.ANY)
    return pl.pallas_call(
        functools.partial(body, table={}),
        name="moe",
        out_shape=jax.ShapeDtypeStruct((8, 4096), F32),
        in_specs=[vmem, vmem, vmem, vmem, hbm, hbm, hbm],
        out_specs=vmem,
        scratch_shapes=[
            pltpu.VMEM((4, 4, 4, 16, XW), BF),
            pltpu.VMEM((8, XW), BF),
            pltpu.VMEM((8, XW), BF),
            pltpu.VMEM((768, 4096), BF),
            pltpu.VMEM((768, 4096), BF),
            pltpu.VMEM((768, 4096), BF),
            pltpu.VMEM((4, 4, 4, 16, 768), F32),
            pltpu.VMEM((4, 4, 4, 16, 768), F32),
            pltpu.VMEM((4, 4, 4, 16, 768), BF),
            pltpu.VMEM((4, 4, 4, 16, 2048), BF),
            pltpu.VMEM((4, 4, 16, 2048), BF),
            pltpu.VMEM((2, 4, 4, 16, 2048), BF),
            pltpu.VMEM((3, 4, 16, 2048), BF),
            pltpu.VMEM((3, 16, 2048), BF),
            pltpu.VMEM((16, 2048), F32),
            pltpu.VMEM((8, 4096), F32),
            pltpu.VMEM((128, 768), BF),
            pltpu.VMEM((16, XW), BF),
            pltpu.SemaphoreType.DMA((112,)),
            pltpu.SemaphoreType.DMA((112,)),
            pltpu.SemaphoreType.DMA((3,)),
        ],
        compiler_params=pltpu.CompilerParams(
            collective_id=0, has_side_effects=True, vmem_limit_bytes=60 << 20
        ),
    )(
        stream_in,
        norm_gain.reshape(1, features),
        expert_ids,
        route_weights,
        w_gate.reshape(hidden, features),
        w_up.reshape(hidden, features),
        w_down.reshape(hidden, features),
    )


def solution(mesh):
    return jax.shard_map(
        local,
        mesh=mesh,
        in_specs=(
            P(("attn", "expert"), None),
            P(),
            P(("attn", "expert"), None),
            P(("attn", "expert"), None),
            P("expert", "attn", None),
            P("expert", "attn", None),
            P("expert", "attn", None),
        ),
        out_specs=P(("attn", "expert"), None),
        check_vma=False,
    )
```

```python
import functools
import jax
import jax.numpy as jnp
from jax import lax
from jax.experimental import pallas as pl
from jax.experimental.pallas import tpu as pltpu
from jax.sharding import PartitionSpec as P

BF = jnp.bfloat16
F32 = jnp.float32
MESH = pl.DeviceIdType.MESH
NT = (((1,), (1,)), ((), ()))

ORDER = ((0, 1, 2), (1, 2, 0), (2, 0, 1))
XW = 4352
HI, LO = 2816, 4224
GSTART, GWIDTH = (0, 1536, 2816), (768, 640, 768)
XK = ((0, 1536), (1536, 1280), (2944, 1280))
WK = ((0, 1536), (1536, 1280), (2816, 1280))
OSTART, OWIDTH, VSTART = (0, 1536, 2816), (768, 640, 640), (0, 768, 1408)
STEPS = (1, -1, 2)


def body(
    x_ref, gain_ref, ids_ref, rw_ref, wg_hbm, wu_hbm, wd_hbm, out_ref,
    X, XB, XS, WG, WU, WD, G, U, A, V, RA, RF, R2, R3, FB, OB, E, ss, rs, wsem, *, table,
):
    attn, expert = lax.axis_index("attn"), lax.axis_index("expert")
    m = (expert // 4, expert % 4, attn // 2)
    c = attn % 2

    def device(axis, step):
        n = [m[0], m[1], m[2]]
        n[axis] = (n[axis] + step + 4) % 4
        return (2 * n[2] + c, 4 * n[0] + n[1])

    sibling = (2 * m[2] + 1 - c, expert)

    def coord(axis, step):
        return (m[axis] + step + 4) % 4

    def copy(key, src, dst, dev):
        number = table.setdefault(key, len(table))
        return pltpu.make_async_remote_copy(
            src_ref=src, dst_ref=dst, send_sem=ss.at[number], recv_sem=rs.at[number],
            device_id=dev, device_id_type=MESH,
        )

    def plane_index(axis, q, half=None):
        idx = [slice(None)] * 3
        idx[axis] = q
        if half is not None:
            idx[0 if axis != 0 else 1] = pl.ds(2 * half, 2)
        return tuple(idx)

    def line_index(along, fixed):
        return tuple(slice(None) if a == along else fixed[a] for a in range(3))

    def gcols(p, core):
        return pl.ds(pl.multiple_of(GSTART[p] + core * GWIDTH[p], 128), GWIDTH[p])

    def ocols(p, core):
        return pl.ds(pl.multiple_of(OSTART[p] + core * OWIDTH[p], 128), OWIDTH[p])

    def vcols(p):
        return pl.ds(VSTART[p], OWIDTH[p])

    loads = [
        pltpu.make_async_copy(h, v, wsem.at[i])
        for i, (h, v) in enumerate(((wg_hbm, WG), (wu_hbm, WU), (wd_hbm, WD)))
    ]
    for load in loads:
        load.start()

    barrier = pltpu.get_barrier_semaphore()
    partners = [sibling] + [device(a, s) for a in range(3) for s in STEPS]
    for dev in partners:
        pl.semaphore_signal(barrier, inc=1, device_id=dev, device_id_type=MESH)

    lane = lax.broadcasted_iota(jnp.int32, (8, 128), 1)
    spread = jnp.zeros((8, 128), F32)
    for k in range(8):
        spread = spread + jnp.where(ids_ref[:, k : k + 1] == lane, rw_ref[:, k : k + 1], 0.0)
    high = spread.astype(BF)
    low = (spread - high.astype(F32)).astype(BF)
    stream = x_ref[...].astype(F32)
    inverse = lax.rsqrt(jnp.sum(stream * stream, axis=-1, keepdims=True) * (1.0 / 4096) + 1e-06)
    normed = (stream * inverse * gain_ref[...].astype(F32).reshape(1, 4096)).astype(BF)
    XB[:, 0:HI] = normed[:, 0:HI]
    XB[:, HI : HI + 128] = high
    XB[:, HI + 128 : LO] = normed[:, HI:4096]
    XB[:, LO:XW] = low

    er = lax.broadcasted_iota(jnp.int32, (128, 768), 0)
    ec = lax.broadcasted_iota(jnp.int32, (128, 768), 1)
    held = er - 4 * expert
    E[...] = jnp.where((ec >= held * 192) & (ec < held * 192 + 192), 1.0, 0.0).astype(BF)

    @pl.loop(0, 16)
    def _(i):
        G[i // 4, i % 4] = jnp.zeros((4, 16, 768), F32)
        U[i // 4, i % 4] = jnp.zeros((4, 16, 768), F32)

    pl.semaphore_wait(barrier, len(partners))
    swap = copy("swap", XB, XS, sibling)
    swap.start()
    swap.wait()
    first = c == 0
    for p in range(3):
        mine, other = XB[:, gcols(p, c)].astype(F32), XS[:, gcols(p, c)].astype(F32)
        rows = jnp.concatenate(
            [jnp.where(first, mine, other), jnp.where(first, other, mine)], axis=0
        )
        X[m[0], m[1], m[2], :, gcols(p, c)] = rows.astype(BF)

    sends = []

    def start(cp):
        cp.start()
        sends.append(cp)

    def landed(key, ref):
        copy(key, ref, ref, sibling).wait_recv()

    def stage1(p):
        a = ORDER[p][0]
        ref = X.at[m[0], m[1], m[2], :, gcols(p, c)]
        for s in STEPS:
            start(copy(("g1", p, s), ref, ref, device(a, s)))

    def stage2(p):
        a, b, _ = ORDER[p]
        for s in STEPS:
            fixed = list(m)
            fixed[a] = coord(a, -s)
            landed(("g1", p, s), X.at[fixed[0], fixed[1], fixed[2], :, gcols(p, c)])
        ref = X.at[line_index(a, m) + (slice(None), gcols(p, c))]
        for s in STEPS:
            start(copy(("g2", p, s), ref, ref, device(b, s)))

    def xplane(p, q, core, half=None):
        return X.at[plane_index(ORDER[p][2], q, half) + (slice(None), gcols(p, core))]

    def stage3(p):
        a, b, k = ORDER[p]
        for s in STEPS:
            fixed = list(m)
            fixed[b] = coord(b, -s)
            landed(("g2", p, s), X.at[line_index(a, fixed) + (slice(None), gcols(p, c))])
        for n in range(2):
            for s, half in ((1, n), (-1, 1 - n)):
                ref = xplane(p, m[k], c, half)
                start(copy(("g3", p, s, half), ref, ref, device(k, s)))
        ref = xplane(p, m[k], c)
        start(copy(("gs", p, 0), ref, ref, sibling))

    def relay(p):
        k = ORDER[p][2]
        for s, half in ((1, 0), (-1, 1)):
            ref = xplane(p, coord(k, -s), c, half)
            landed(("g3", p, s, half), ref)
            start(copy(("gr", p, s), ref, ref, device(k, s)))

    def share(p):
        k = ORDER[p][2]
        for s, half in ((1, 1), (-1, 0)):
            landed(("g3", p, s, half), xplane(p, coord(k, -s), c, half))
            ref = xplane(p, coord(k, -s), c)
            start(copy(("gs", p, s), ref, ref, sibling))

    def share_far(p):
        k = ORDER[p][2]
        for s, half in ((1, 0), (-1, 1)):
            landed(("gr", p, s), xplane(p, coord(k, 2), c, half))
        ref = xplane(p, coord(k, 2), c)
        start(copy(("gs", p, 2), ref, ref, sibling))

    def unit(p, s):
        k = ORDER[p][2]
        q = coord(k, -s)
        landed(("gs", p, s), xplane(p, q, 1 - c))
        index = plane_index(k, q)
        x0, xn = XK[p]
        w0, wn = WK[p]

        xs = X[index + (slice(None), slice(x0, x0 + xn))].reshape(256, xn)
        for w, acc in ((WG, G), (WU, U)):
            r = lax.dot_general(xs, w[:, w0 : w0 + wn], NT, preferred_element_type=F32)
            acc[index] += r.reshape(4, 4, 16, 768)

    for p in range(3):
        stage1(p)

    for p in range(3):
        stage2(p)
    for p in range(3):
        stage3(p)
    loads[0].wait()
    loads[1].wait()
    for p in range(3):
        unit(p, 0)
    for p in range(3):
        relay(p)
    for p in range(3):
        share(p)
    for p in range(3):
        unit(p, 1)
    unit(0, -1)
    unit(1, -1)
    for p in range(3):
        share_far(p)
    unit(2, -1)
    for p in range(3):
        unit(p, 2)
    loads[2].wait()
    for cp in sends:
        cp.wait_send()
    sends.clear()

    @pl.loop(0, 4)
    def _(i):
        g = G[i].reshape(256, 768)
        u = U[i].reshape(256, 768)
        hi = X[i, :, :, :, HI : HI + 128].reshape(256, 128)
        lo = X[i, :, :, :, LO:XW].reshape(256, 128)
        w = jnp.dot(hi, E[...], preferred_element_type=F32) + jnp.dot(
            lo, E[...], preferred_element_type=F32
        )
        A[i] = (g / (1.0 + jnp.exp(-g)) * u * w).astype(BF).reshape(4, 4, 16, 768)

    def down(p, s):
        k = ORDER[p][2]
        q = coord(k, s)
        index = plane_index(k, q)
        cs = slice(OSTART[p], OSTART[p] + 2 * OWIDTH[p])
        r = jnp.dot(A[index].reshape(256, 768), WD[:, cs], preferred_element_type=F32)
        X[index + (slice(None), cs)] = r.astype(BF).reshape(4, 4, 16, 2 * OWIDTH[p])

        start(
            copy(
                ("rs", p, s),
                X.at[index + (slice(None), ocols(p, 1 - c))],
                V.at[index + (slice(None), vcols(p))],
                sibling,
            )
        )

    def row_index(axis, q, i):
        rest = [a for a in range(3) if a != axis]
        idx = [None] * 3
        idx[axis] = q
        idx[rest[0]] = i
        idx[rest[1]] = slice(None)
        return tuple(idx)

    def paired(p, s):
        k = ORDER[p][2]
        q = coord(k, s)
        landed(("rs", p, s), V.at[plane_index(k, q) + (slice(None), vcols(p))])

        @pl.loop(0, 4)
        def _(i):
            at = row_index(k, q, i)
            o = at + (slice(None), ocols(p, c))
            X[o] = (X[o].astype(F32) + V[at + (slice(None), vcols(p))].astype(F32)).astype(BF)

    def oplane(p, q, half=None):
        return X.at[plane_index(ORDER[p][2], q, half) + (slice(None), ocols(p, c))]

    def send_far(p):
        k = ORDER[p][2]
        for s, half in ((1, 0), (-1, 1)):
            start(
                copy(
                    ("ra", p, s), oplane(p, coord(k, 2), half),
                    RA.at[pl.ds(2 * half, 2), :, :, vcols(p)], device(k, s),
                )
            )

    def send_half(p, s, half):
        k = ORDER[p][2]
        slot = 0 if s == 1 else 1
        start(
            copy(
                ("rf", p, s, half), oplane(p, coord(k, s), half),
                RF.at[slot, pl.ds(2 * half, 2), :, :, vcols(p)], device(k, s),
            )
        )

    def relay_back(p):
        k = ORDER[p][2]
        for s, half in ((1, 0), (-1, 1)):
            landed(("ra", p, s), RA.at[pl.ds(2 * half, 2), :, :, vcols(p)])
            q = coord(k, s)

            @pl.loop(2 * half, 2 * half + 2)
            def _(i):
                o = row_index(k, q, i) + (slice(None), ocols(p, c))
                X[o] = (X[o].astype(F32) + RA[i, :, :, vcols(p)].astype(F32)).astype(BF)

            send_half(p, s, half)

    def gather_planes(p):
        a, b, k = ORDER[p]
        for s in (1, -1):
            for half in range(2):
                slot = 0 if s == 1 else 1
                landed(("rf", p, s, half), RF.at[slot, pl.ds(2 * half, 2), :, :, vcols(p)])

        @pl.loop(0, 4)
        def _(i):
            o = row_index(k, m[k], i) + (slice(None), ocols(p, c))
            X[o] = (
                X[o].astype(F32)
                + RF[0, i, :, :, vcols(p)].astype(F32)
                + RF[1, i, :, :, vcols(p)].astype(F32)
            ).astype(BF)

        for n, s in enumerate(STEPS):
            fixed = list(m)
            fixed[b] = coord(b, s)
            start(
                copy(
                    ("r2", p, s), X.at[line_index(a, fixed) + (slice(None), ocols(p, c))],
                    R2.at[n, :, :, vcols(p)], device(b, s),
                )
            )

    def gather_lines(p):
        a = ORDER[p][0]
        for n, s in enumerate(STEPS):
            landed(("r2", p, s), R2.at[n, :, :, vcols(p)])
        o = line_index(a, m) + (slice(None), ocols(p, c))
        total = X[o].astype(F32)
        for n in range(3):
            total = total + R2[n, :, :, vcols(p)].astype(F32)
        X[o] = total.astype(BF)
        for n, s in enumerate(STEPS):
            fixed = list(m)
            fixed[a] = coord(a, s)
            start(
                copy(
                    ("r3", p, s), X.at[fixed[0], fixed[1], fixed[2], :, ocols(p, c)],
                    R3.at[n, :, vcols(p)], device(a, s),
                )
            )

    def gather_blocks(p):
        for n, s in enumerate(STEPS):
            landed(("r3", p, s), R3.at[n, :, vcols(p)])
        total = X[m[0], m[1], m[2], :, ocols(p, c)].astype(F32)
        for n in range(3):
            total = total + R3[n, :, vcols(p)].astype(F32)
        FB[:, vcols(p)] = total
        start(
            copy(
                ("r4", p), FB.at[pl.ds(pl.multiple_of(8 * (1 - c), 8), 8), vcols(p)],
                OB.at[:, ocols(p, c)], sibling,
            )
        )
        OB[:, ocols(p, c)] = FB[pl.ds(pl.multiple_of(8 * c, 8), 8), vcols(p)]

    for p in range(3):
        down(p, 2)
    for p in range(3):
        down(p, 1)
        paired(p, 2)
        send_far(p)
    for p in range(3):
        down(p, -1)
        paired(p, 1)
        send_half(p, 1, 1)
    for p in range(3):
        down(p, 0)
        paired(p, -1)
        send_half(p, -1, 0)
    for p in range(3):
        relay_back(p)
    for p in range(3):
        paired(p, 0)
    for p in range(3):
        gather_planes(p)
    for p in range(3):
        gather_lines(p)
    for p in range(3):
        gather_blocks(p)
    for p in range(3):
        landed(("r4", p), OB.at[:, ocols(p, 1 - c)])
    out_ref[...] = OB[...]
    for cp in sends:
        cp.wait_send()


def local(stream_in, norm_gain, expert_ids, route_weights, w_gate, w_up, w_down):
    hidden, features = w_gate.shape[0] * w_gate.shape[1], w_gate.shape[2]
    vmem = pl.BlockSpec(memory_space=pltpu.VMEM)
    hbm = pl.BlockSpec(memory_space=pl.ANY)
    return pl.pallas_call(
        functools.partial(body, table={}),
        name="moe",
        out_shape=jax.ShapeDtypeStruct((8, 4096), F32),
        in_specs=[vmem, vmem, vmem, vmem, hbm, hbm, hbm],
        out_specs=vmem,
        scratch_shapes=[
            pltpu.VMEM((4, 4, 4, 16, XW), BF),
            pltpu.VMEM((8, XW), BF),
            pltpu.VMEM((8, XW), BF),
            pltpu.VMEM((768, 4096), BF),
            pltpu.VMEM((768, 4096), BF),
            pltpu.VMEM((768, 4096), BF),
            pltpu.VMEM((4, 4, 4, 16, 768), F32),
            pltpu.VMEM((4, 4, 4, 16, 768), F32),
            pltpu.VMEM((4, 4, 4, 16, 768), BF),
            pltpu.VMEM((4, 4, 4, 16, 2048), BF),
            pltpu.VMEM((4, 4, 16, 2048), BF),
            pltpu.VMEM((2, 4, 4, 16, 2048), BF),
            pltpu.VMEM((3, 4, 16, 2048), BF),
            pltpu.VMEM((3, 16, 2048), BF),
            pltpu.VMEM((16, 2048), F32),
            pltpu.VMEM((8, 4096), F32),
            pltpu.VMEM((128, 768), BF),
            pltpu.SemaphoreType.DMA((112,)),
            pltpu.SemaphoreType.DMA((112,)),
            pltpu.SemaphoreType.DMA((3,)),
        ],
        compiler_params=pltpu.CompilerParams(
            collective_id=0, has_side_effects=True, vmem_limit_bytes=60 << 20
        ),
    )(
        stream_in,
        norm_gain,
        expert_ids,
        route_weights,
        w_gate.reshape(hidden, features),
        w_up.reshape(hidden, features),
        w_down.reshape(hidden, features),
    )


def solution(mesh):
    return jax.shard_map(
        local,
        mesh=mesh,
        in_specs=(
            P(("attn", "expert"), None),
            P(),
            P(("attn", "expert"), None),
            P(("attn", "expert"), None),
            P("expert", "attn", None),
            P("expert", "attn", None),
            P("expert", "attn", None),
        ),
        out_specs=P(("attn", "expert"), None),
        check_vma=False,
    )
```

```python
import functools
import jax
import jax.numpy as jnp
from jax import lax
from jax.experimental import pallas as pl
from jax.experimental.pallas import tpu as pltpu
from jax.sharding import PartitionSpec as P

BF = jnp.bfloat16
F32 = jnp.float32
MESH = pl.DeviceIdType.MESH
NT = (((1,), (1,)), ((), ()))

ORDER = ((0, 1, 2), (1, 2, 0), (2, 0, 1))
XW = 4352
HI, LO = 2816, 4224
GSTART, GWIDTH = (0, 1536, 2816), (768, 640, 768)
XK = ((0, 1536), (1536, 1280), (2944, 1280))
WK = ((0, 1536), (1536, 1280), (2816, 1280))
OSTART, OWIDTH, VSTART = (0, 1536, 2816), (768, 640, 640), (0, 768, 1408)
STEPS = (1, -1, 2)


def body(
    x_ref, gain_ref, ids_ref, rw_ref, wg_hbm, wu_hbm, wd_hbm, out_ref,
    X, XB, XS, WG, WU, WD, G, U, A, V, RA, RF, R2, R3, FB, OB, E, ss, rs, wsem, *, table,
):
    attn, expert = lax.axis_index("attn"), lax.axis_index("expert")
    m = (expert // 4, expert % 4, attn // 2)
    c = attn % 2

    def device(axis, step):
        n = [m[0], m[1], m[2]]
        n[axis] = (n[axis] + step + 4) % 4
        return (2 * n[2] + c, 4 * n[0] + n[1])

    sibling = (2 * m[2] + 1 - c, expert)

    def coord(axis, step):
        return (m[axis] + step + 4) % 4

    def copy(key, src, dst, dev):
        number = table.setdefault(key, len(table))
        return pltpu.make_async_remote_copy(
            src_ref=src, dst_ref=dst, send_sem=ss.at[number], recv_sem=rs.at[number],
            device_id=dev, device_id_type=MESH,
        )

    def plane_index(axis, q):
        idx = [slice(None)] * 3
        idx[axis] = q
        return tuple(idx)

    def line_at(p, b_step, k_step):
        a, b, k = ORDER[p]
        idx = [slice(None)] * 3
        idx[b], idx[k] = coord(b, b_step), coord(k, k_step)
        return tuple(idx) + (slice(None),)

    def gcols(p, core):
        return pl.ds(pl.multiple_of(GSTART[p] + core * GWIDTH[p], 128), GWIDTH[p])

    def ocols(p, core):
        return pl.ds(pl.multiple_of(OSTART[p] + core * OWIDTH[p], 128), OWIDTH[p])

    def vcols(p):
        return pl.ds(VSTART[p], OWIDTH[p])

    loads = [
        pltpu.make_async_copy(h, v, wsem.at[i])
        for i, (h, v) in enumerate(((wg_hbm, WG), (wu_hbm, WU), (wd_hbm, WD)))
    ]
    for load in loads:
        load.start()

    barrier = pltpu.get_barrier_semaphore()
    partners = [sibling] + [device(a, s) for a in range(3) for s in STEPS]
    for dev in partners:
        pl.semaphore_signal(barrier, inc=1, device_id=dev, device_id_type=MESH)

    lane = lax.broadcasted_iota(jnp.int32, (8, 128), 1)
    spread = jnp.zeros((8, 128), F32)
    for k in range(8):
        spread = spread + jnp.where(ids_ref[:, k : k + 1] == lane, rw_ref[:, k : k + 1], 0.0)
    high = spread.astype(BF)
    low = (spread - high.astype(F32)).astype(BF)
    stream = x_ref[...].astype(F32)
    inverse = lax.rsqrt(jnp.sum(stream * stream, axis=-1, keepdims=True) * (1.0 / 4096) + 1e-06)
    normed = (stream * inverse * gain_ref[...].astype(F32).reshape(1, 4096)).astype(BF)
    XB[:, 0:HI] = normed[:, 0:HI]
    XB[:, HI : HI + 128] = high
    XB[:, HI + 128 : LO] = normed[:, HI:4096]
    XB[:, LO:XW] = low

    er = lax.broadcasted_iota(jnp.int32, (128, 768), 0)
    ec = lax.broadcasted_iota(jnp.int32, (128, 768), 1)
    held = er - 4 * expert
    E[...] = jnp.where((ec >= held * 192) & (ec < held * 192 + 192), 1.0, 0.0).astype(BF)

    @pl.loop(0, 16)
    def _(i):
        G[i // 4, i % 4] = jnp.zeros((4, 16, 768), F32)
        U[i // 4, i % 4] = jnp.zeros((4, 16, 768), F32)

    pl.semaphore_wait(barrier, len(partners))
    swap = copy("swap", XB, XS, sibling)
    swap.start()
    swap.wait()
    first = c == 0
    for p in range(3):
        mine, other = XB[:, gcols(p, c)].astype(F32), XS[:, gcols(p, c)].astype(F32)
        rows = jnp.concatenate(
            [jnp.where(first, mine, other), jnp.where(first, other, mine)], axis=0
        )
        X[m[0], m[1], m[2], :, gcols(p, c)] = rows.astype(BF)

    sends = []

    def start(cp):
        cp.start()
        sends.append(cp)

    def landed(key, ref):
        copy(key, ref, ref, sibling).wait_recv()

    def gline(p, b_step, k_step):
        return X.at[line_at(p, b_step, k_step) + (gcols(p, c),)]

    def send_line(p, s, b_step):
        start(
            copy(
                ("g3", p, s, b_step), gline(p, b_step, 0), gline(p, b_step, 0),
                device(ORDER[p][2], s),
            )
        )

    def stage1(p):
        a = ORDER[p][0]
        ref = X.at[m[0], m[1], m[2], :, gcols(p, c)]
        for s in STEPS:
            start(copy(("g1", p, s), ref, ref, device(a, s)))

    def stage2(p):
        a, b, _ = ORDER[p]
        for s in STEPS:
            fixed = list(m)
            fixed[a] = coord(a, -s)
            landed(("g1", p, s), X.at[fixed[0], fixed[1], fixed[2], :, gcols(p, c)])
        ref = gline(p, 0, 0)
        for s in STEPS:
            start(copy(("g2", p, s), ref, ref, device(b, s)))

    def xplane(p, q, core):
        return X.at[plane_index(ORDER[p][2], q) + (slice(None), gcols(p, core))]

    def stage3(p):
        k = ORDER[p][2]
        for s in STEPS:
            landed(("g2", p, s), gline(p, -s, 0))
        for n in (1, 2, 3):
            send_line(p, 1, n)
            send_line(p, -1, 4 - n)
        ref = xplane(p, m[k], c)
        start(copy(("gs", p, 0), ref, ref, sibling))

    def relay(p, s, b_step):
        ref = gline(p, b_step, -s)
        landed(("g3", p, s, b_step), ref)
        start(copy(("gr", p, s, b_step), ref, ref, device(ORDER[p][2], s)))

    def share(p):
        k = ORDER[p][2]
        for s, lines in ((1, (2, 3)), (-1, (1, 0))):
            for n in lines:
                landed(("g3", p, s, n), gline(p, n, -s))
            ref = xplane(p, coord(k, -s), c)
            start(copy(("gs", p, s), ref, ref, sibling))

    def share_far(p):
        for s, n in ((1, 0), (-1, 3), (1, 1), (-1, 2)):
            ref = gline(p, n, 2)
            landed(("gr", p, s, n), ref)
            start(copy(("gl", p, n), ref, ref, sibling))

    def unit(p, s):
        k = ORDER[p][2]
        q = coord(k, -s)
        if s == 2:
            for n in range(4):
                landed(("gl", p, n), X.at[line_at(p, n, 2) + (gcols(p, 1 - c),)])
        else:
            landed(("gs", p, s), xplane(p, q, 1 - c))
        index = plane_index(k, q)
        x0, xn = XK[p]
        w0, wn = WK[p]

        xs = X[index + (slice(None), slice(x0, x0 + xn))].reshape(256, xn)
        for w, acc in ((WG, G), (WU, U)):
            r = lax.dot_general(xs, w[:, w0 : w0 + wn], NT, preferred_element_type=F32)
            acc[index] += r.reshape(4, 4, 16, 768)

    for p in range(3):
        stage1(p)

    for p in range(3):
        stage2(p)
    for p in range(3):
        send_line(p, 1, 0)
        send_line(p, -1, 0)
    for p in range(3):
        stage3(p)
    for p in range(3):
        relay(p, 1, 0)
    loads[0].wait()
    loads[1].wait()
    for p in range(3):
        unit(p, 0)
    for p in range(3):
        relay(p, -1, 3)
        relay(p, 1, 1)
    for p in range(3):
        relay(p, -1, 2)
    for p in range(3):
        share(p)
    for p in range(3):
        unit(p, 1)
    for p in range(3):
        share_far(p)
    for p in range(3):
        unit(p, -1)
    for p in range(3):
        unit(p, 2)
    loads[2].wait()
    for cp in sends:
        cp.wait_send()
    sends.clear()

    @pl.loop(0, 4)
    def _(i):
        g = G[i].reshape(256, 768)
        u = U[i].reshape(256, 768)
        hi = X[i, :, :, :, HI : HI + 128].reshape(256, 128)
        lo = X[i, :, :, :, LO:XW].reshape(256, 128)
        w = jnp.dot(hi, E[...], preferred_element_type=F32) + jnp.dot(
            lo, E[...], preferred_element_type=F32
        )
        A[i] = (g / (1.0 + jnp.exp(-g)) * u * w).astype(BF).reshape(4, 4, 16, 768)

    def down(p, s):
        k = ORDER[p][2]
        q = coord(k, s)
        index = plane_index(k, q)
        cs = slice(OSTART[p], OSTART[p] + 2 * OWIDTH[p])
        r = jnp.dot(A[index].reshape(256, 768), WD[:, cs], preferred_element_type=F32)
        X[index + (slice(None), cs)] = r.astype(BF).reshape(4, 4, 16, 2 * OWIDTH[p])

        start(
            copy(
                ("rs", p, s),
                X.at[index + (slice(None), ocols(p, 1 - c))],
                V.at[index + (slice(None), vcols(p))],
                sibling,
            )
        )

    def row_index(axis, q, i):
        rest = [a for a in range(3) if a != axis]
        idx = [None] * 3
        idx[axis] = q
        idx[rest[0]] = i
        idx[rest[1]] = slice(None)
        return tuple(idx)

    def paired(p, s):
        k = ORDER[p][2]
        q = coord(k, s)
        landed(("rs", p, s), V.at[plane_index(k, q) + (slice(None), vcols(p))])

        @pl.loop(0, 4)
        def _(i):
            at = row_index(k, q, i)
            o = at + (slice(None), ocols(p, c))
            X[o] = (X[o].astype(F32) + V[at + (slice(None), vcols(p))].astype(F32)).astype(BF)

    def oline(p, b_step, k_step):
        return line_at(p, b_step, k_step) + (ocols(p, c),)

    def send_far(p):
        for s, n in ((1, 1), (-1, 3), (1, 2), (-1, 0)):
            start(
                copy(
                    ("ra", p, s, n), X.at[oline(p, n, 2)], RA.at[n, :, :, vcols(p)],
                    device(ORDER[p][2], s),
                )
            )

    def send_near(p, s, n):
        start(
            copy(
                ("rf", p, s, n), X.at[oline(p, n, s)],
                RF.at[0 if s == 1 else 1, n, :, :, vcols(p)], device(ORDER[p][2], s),
            )
        )

    def relay_back(p, s, n):
        landed(("ra", p, s, n), RA.at[n, :, :, vcols(p)])
        o = oline(p, n, s)
        X[o] = (X[o].astype(F32) + RA[n, :, :, vcols(p)].astype(F32)).astype(BF)
        send_near(p, s, n)

    def ring_total(p, n):
        for slot, s in ((0, 1), (1, -1)):
            landed(("rf", p, s, n), RF.at[slot, n, :, :, vcols(p)])
        return (
            X[oline(p, n, 0)].astype(F32)
            + RF[0, n, :, :, vcols(p)].astype(F32)
            + RF[1, n, :, :, vcols(p)].astype(F32)
        )

    def pass_line(p, n):
        X[oline(p, n, 0)] = ring_total(p, n).astype(BF)
        start(
            copy(
                ("r2", p, n), X.at[oline(p, n, 0)], R2.at[n - 1, :, :, vcols(p)],
                device(ORDER[p][1], n),
            )
        )

    def own_line(p):
        X[oline(p, 0, 0)] = ring_total(p, 0).astype(BF)

    def gather_lines(p):
        a = ORDER[p][0]
        for n in range(3):
            landed(("r2", p, n + 1), R2.at[n, :, :, vcols(p)])
        o = oline(p, 0, 0)
        total = X[o].astype(F32)
        for n in range(3):
            total = total + R2[n, :, :, vcols(p)].astype(F32)
        X[o] = total.astype(BF)
        for n, s in enumerate(STEPS):
            fixed = list(m)
            fixed[a] = coord(a, s)
            start(
                copy(
                    ("r3", p, s), X.at[fixed[0], fixed[1], fixed[2], :, ocols(p, c)],
                    R3.at[n, :, vcols(p)], device(a, s),
                )
            )

    def gather_blocks(p):
        for n, s in enumerate(STEPS):
            landed(("r3", p, s), R3.at[n, :, vcols(p)])
        total = X[m[0], m[1], m[2], :, ocols(p, c)].astype(F32)
        for n in range(3):
            total = total + R3[n, :, vcols(p)].astype(F32)
        FB[:, vcols(p)] = total
        start(
            copy(
                ("r4", p), FB.at[pl.ds(pl.multiple_of(8 * (1 - c), 8), 8), vcols(p)],
                OB.at[:, ocols(p, c)], sibling,
            )
        )
        OB[:, ocols(p, c)] = FB[pl.ds(pl.multiple_of(8 * c, 8), 8), vcols(p)]

    for p in range(3):
        down(p, 2)
    for p in range(3):
        down(p, 1)
        paired(p, 2)
        send_far(p)
    for p in range(3):
        down(p, -1)
        paired(p, 1)
        send_near(p, 1, 3)
    for p in range(3):
        down(p, 0)
        paired(p, -1)
        send_near(p, -1, 1)
        send_near(p, -1, 2)
    for p in range(3):
        paired(p, 0)
    for p in range(3):
        relay_back(p, 1, 1)
        relay_back(p, -1, 3)
    for p in range(3):
        relay_back(p, 1, 2)
        relay_back(p, -1, 0)
        send_near(p, 1, 0)
    for n in (1, 2, 3):
        for p in range(3):
            pass_line(p, n)
    for p in range(3):
        own_line(p)
    for p in range(3):
        gather_lines(p)
    for p in range(3):
        gather_blocks(p)
    for p in range(3):
        landed(("r4", p), OB.at[:, ocols(p, 1 - c)])
    out_ref[...] = OB[...]
    for cp in sends:
        cp.wait_send()


def local(stream_in, norm_gain, expert_ids, route_weights, w_gate, w_up, w_down):
    hidden, features = w_gate.shape[0] * w_gate.shape[1], w_gate.shape[2]
    vmem = pl.BlockSpec(memory_space=pltpu.VMEM)
    hbm = pl.BlockSpec(memory_space=pl.ANY)
    return pl.pallas_call(
        functools.partial(body, table={}),
        name="moe",
        out_shape=jax.ShapeDtypeStruct((8, 4096), F32),
        in_specs=[vmem, vmem, vmem, vmem, hbm, hbm, hbm],
        out_specs=vmem,
        scratch_shapes=[
            pltpu.VMEM((4, 4, 4, 16, XW), BF),
            pltpu.VMEM((8, XW), BF),
            pltpu.VMEM((8, XW), BF),
            pltpu.VMEM((768, 4096), BF),
            pltpu.VMEM((768, 4096), BF),
            pltpu.VMEM((768, 4096), BF),
            pltpu.VMEM((4, 4, 4, 16, 768), F32),
            pltpu.VMEM((4, 4, 4, 16, 768), F32),
            pltpu.VMEM((4, 4, 4, 16, 768), BF),
            pltpu.VMEM((4, 4, 4, 16, 2048), BF),
            pltpu.VMEM((4, 4, 16, 2048), BF),
            pltpu.VMEM((2, 4, 4, 16, 2048), BF),
            pltpu.VMEM((3, 4, 16, 2048), BF),
            pltpu.VMEM((3, 16, 2048), BF),
            pltpu.VMEM((16, 2048), F32),
            pltpu.VMEM((8, 4096), F32),
            pltpu.VMEM((128, 768), BF),
            pltpu.SemaphoreType.DMA((192,)),
            pltpu.SemaphoreType.DMA((192,)),
            pltpu.SemaphoreType.DMA((3,)),
        ],
        compiler_params=pltpu.CompilerParams(
            collective_id=0, has_side_effects=True, vmem_limit_bytes=60 << 20
        ),
    )(
        stream_in,
        norm_gain,
        expert_ids,
        route_weights,
        w_gate.reshape(hidden, features),
        w_up.reshape(hidden, features),
        w_down.reshape(hidden, features),
    )


def solution(mesh):
    return jax.shard_map(
        local,
        mesh=mesh,
        in_specs=(
            P(("attn", "expert"), None),
            P(),
            P(("attn", "expert"), None),
            P(("attn", "expert"), None),
            P("expert", "attn", None),
            P("expert", "attn", None),
            P("expert", "attn", None),
        ),
        out_specs=P(("attn", "expert"), None),
        check_vma=False,
    )
```

```python
import functools
import jax
import jax.numpy as jnp
from jax import lax
from jax.experimental import pallas as pl
from jax.experimental.pallas import tpu as pltpu
from jax.sharding import PartitionSpec as P

BF = jnp.bfloat16
F32 = jnp.float32
MESH = pl.DeviceIdType.MESH
NT = (((1,), (1,)), ((), ()))

ORDER = ((0, 1, 2), (1, 2, 0), (2, 0, 1))
XW = 4352
HI, LO = 2816, 4224
GSTART, GWIDTH = (0, 1536, 2816), (768, 640, 768)
XK = ((0, 1536), (1536, 1280), (2944, 1280))
WK = ((0, 1536), (1536, 1280), (2816, 1280))
OSTART, OWIDTH, VSTART = (0, 1536, 2816), (768, 640, 640), (0, 768, 1408)
STEPS = (1, -1, 2)


def body(
    x_ref, gain_ref, ids_ref, rw_ref, wg_hbm, wu_hbm, wd_hbm, out_ref,
    X, XB, XS, WG, WU, WD, G, U, A, V, RA, RF, R2, R3, FB, OB, E, ss, rs, wsem, *, table,
):
    attn, expert = lax.axis_index("attn"), lax.axis_index("expert")
    m = (expert // 4, expert % 4, attn // 2)
    c = attn % 2

    def device(axis, step):
        n = [m[0], m[1], m[2]]
        n[axis] = (n[axis] + step + 4) % 4
        return (2 * n[2] + c, 4 * n[0] + n[1])

    sibling = (2 * m[2] + 1 - c, expert)

    def coord(axis, step):
        return (m[axis] + step + 4) % 4

    def copy(key, src, dst, dev):
        number = table.setdefault(key, len(table))
        return pltpu.make_async_remote_copy(
            src_ref=src, dst_ref=dst, send_sem=ss.at[number], recv_sem=rs.at[number],
            device_id=dev, device_id_type=MESH,
        )

    def plane_index(axis, q):
        idx = [slice(None)] * 3
        idx[axis] = q
        return tuple(idx)

    def line_at(p, b_step, k_step):
        a, b, k = ORDER[p]
        idx = [slice(None)] * 3
        idx[b], idx[k] = coord(b, b_step), coord(k, k_step)
        return tuple(idx) + (slice(None),)

    def gcols(p, core):
        return pl.ds(pl.multiple_of(GSTART[p] + core * GWIDTH[p], 128), GWIDTH[p])

    def ocols(p, core):
        return pl.ds(pl.multiple_of(OSTART[p] + core * OWIDTH[p], 128), OWIDTH[p])

    def vcols(p):
        return pl.ds(VSTART[p], OWIDTH[p])

    loads = [
        pltpu.make_async_copy(h, v, wsem.at[i])
        for i, (h, v) in enumerate(((wg_hbm, WG), (wu_hbm, WU), (wd_hbm, WD)))
    ]
    for load in loads:
        load.start()

    barrier = pltpu.get_barrier_semaphore()
    def across(dev):
        return (dev[0] + 1 - 2 * c, dev[1])

    partners = [sibling]
    for a in range(3):
        for s in STEPS:
            partners += [device(a, s), across(device(a, s))]
    for dev in partners:
        pl.semaphore_signal(barrier, inc=1, device_id=dev, device_id_type=MESH)

    lane = lax.broadcasted_iota(jnp.int32, (8, 128), 1)
    spread = jnp.zeros((8, 128), F32)
    for k in range(8):
        spread = spread + jnp.where(ids_ref[:, k : k + 1] == lane, rw_ref[:, k : k + 1], 0.0)
    high = spread.astype(BF)
    low = (spread - high.astype(F32)).astype(BF)
    stream = x_ref[...].astype(F32)
    inverse = lax.rsqrt(jnp.sum(stream * stream, axis=-1, keepdims=True) * (1.0 / 4096) + 1e-06)
    normed = (stream * inverse * gain_ref[...].astype(F32).reshape(1, 4096)).astype(BF)
    XB[:, 0:HI] = normed[:, 0:HI]
    XB[:, HI : HI + 128] = high
    XB[:, HI + 128 : LO] = normed[:, HI:4096]
    XB[:, LO:XW] = low

    er = lax.broadcasted_iota(jnp.int32, (128, 768), 0)
    ec = lax.broadcasted_iota(jnp.int32, (128, 768), 1)
    held = er - 4 * expert
    E[...] = jnp.where((ec >= held * 192) & (ec < held * 192 + 192), 1.0, 0.0).astype(BF)

    @pl.loop(0, 16)
    def _(i):
        G[i // 4, i % 4] = jnp.zeros((4, 16, 768), F32)
        U[i // 4, i % 4] = jnp.zeros((4, 16, 768), F32)

    pl.semaphore_wait(barrier, len(partners))
    sends = []

    def start(cp):
        cp.start()
        sends.append(cp)

    def landed(key, ref):
        copy(key, ref, ref, sibling).wait_recv()

    def gline(p, b_step, k_step):
        return X.at[line_at(p, b_step, k_step) + (gcols(p, c),)]

    def send_line(p, s, b_step):
        start(
            copy(
                ("g3", p, s, b_step), gline(p, b_step, 0), gline(p, b_step, 0),
                device(ORDER[p][2], s),
            )
        )

    def stage1(p):
        a = ORDER[p][0]
        mine, other = gcols(p, c), gcols(p, 1 - c)
        start(copy(("g0", p), XB.at[:, other], XS.at[0, c, :, other], sibling))
        for i, s in enumerate(STEPS):
            dev = device(a, s)
            start(copy(("g1", p, s, 0), XB.at[:, mine], XS.at[i + 1, c, :, mine], dev))
            start(copy(("g1", p, s, 1), XB.at[:, other], XS.at[i + 1, c, :, other], across(dev)))

    def gblock(p, b_step, a_step):
        a, b, _ = ORDER[p]
        n = list(m)
        n[a], n[b] = coord(a, a_step), coord(b, b_step)
        return (n[0], n[1], n[2], slice(None), gcols(p, c))

    def stage2(p, i):
        b = ORDER[p][1]
        mine = gcols(p, c)
        if i == 0:
            XS[0, c, :, mine] = XB[:, mine]
            landed(("g0", p), XS.at[0, 1 - c, :, mine])
            a_step = 0
        else:
            a_step = -STEPS[i - 1]
            landed(("g1", p, STEPS[i - 1], 0), XS.at[i, c, :, mine])
            landed(("g1", p, STEPS[i - 1], 1), XS.at[i, 1 - c, :, mine])
        rows = jnp.concatenate(
            [XS[i, 0, :, mine].astype(F32), XS[i, 1, :, mine].astype(F32)], axis=0
        )
        X[gblock(p, 0, a_step)] = rows.astype(BF)
        ref = X.at[gblock(p, 0, a_step)]
        for s in STEPS:
            start(copy(("g2", p, s, i), ref, ref, device(b, s)))

    def xplane(p, q, core):
        return X.at[plane_index(ORDER[p][2], q) + (slice(None), gcols(p, core))]

    def stage3(p):
        k = ORDER[p][2]
        for i in range(4):
            for s in STEPS:
                a_step = 0 if i == 0 else -STEPS[i - 1]
                landed(("g2", p, s, i), X.at[gblock(p, -s, a_step)])
        for n in (1, 2, 3):
            send_line(p, 1, n)
            send_line(p, -1, 4 - n)
        ref = xplane(p, m[k], c)
        start(copy(("gs", p, 0), ref, ref, sibling))

    def relay(p, s, b_step):
        ref = gline(p, b_step, -s)
        landed(("g3", p, s, b_step), ref)
        start(copy(("gr", p, s, b_step), ref, ref, device(ORDER[p][2], s)))
        start(copy(("gl", p, s, b_step), ref, ref, sibling))

    def share(p, s, b_step):
        ref = gline(p, b_step, -s)
        landed(("g3", p, s, b_step), ref)
        start(copy(("gl", p, s, b_step), ref, ref, sibling))

    def share_far(p):
        for s, n in ((1, 0), (-1, 3), (1, 1), (-1, 2)):
            ref = gline(p, n, 2)
            landed(("gr", p, s, n), ref)
            start(copy(("gl", p, 2, n), ref, ref, sibling))

    def unit(p, s):
        k = ORDER[p][2]
        q = coord(k, -s)
        if s == 0:
            landed(("gs", p, 0), xplane(p, q, 1 - c))
        else:
            for n in range(4):
                landed(("gl", p, s, n), X.at[line_at(p, n, -s) + (gcols(p, 1 - c),)])
        index = plane_index(k, q)
        x0, xn = XK[p]
        w0, wn = WK[p]

        xs = X[index + (slice(None), slice(x0, x0 + xn))].reshape(256, xn)
        for w, acc in ((WG, G), (WU, U)):
            r = lax.dot_general(xs, w[:, w0 : w0 + wn], NT, preferred_element_type=F32)
            acc[index] += r.reshape(4, 4, 16, 768)

    for p in range(3):
        stage1(p)

    for i in range(4):
        for p in range(3):
            stage2(p, i)
    for p in range(3):
        send_line(p, 1, 0)
        send_line(p, -1, 0)
    for p in range(3):
        stage3(p)
    for p in range(3):
        relay(p, 1, 0)
        share(p, -1, 0)
    loads[0].wait()
    loads[1].wait()
    for p in range(3):
        unit(p, 0)
    for p in range(3):
        relay(p, -1, 3)
        relay(p, 1, 1)
    for p in range(3):
        relay(p, -1, 2)
        share(p, 1, 2)
    for p in range(3):
        share(p, 1, 3)
        share(p, -1, 1)
    for p in range(3):
        unit(p, 1)
    for p in range(3):
        share_far(p)
    for p in range(3):
        unit(p, -1)
    for p in range(3):
        unit(p, 2)
    loads[2].wait()
    for cp in sends:
        cp.wait_send()
    sends.clear()

    @pl.loop(0, 4)
    def _(i):
        g = G[i].reshape(256, 768)
        u = U[i].reshape(256, 768)
        hi = X[i, :, :, :, HI : HI + 128].reshape(256, 128)
        lo = X[i, :, :, :, LO:XW].reshape(256, 128)
        w = jnp.dot(hi, E[...], preferred_element_type=F32) + jnp.dot(
            lo, E[...], preferred_element_type=F32
        )
        A[i] = (g / (1.0 + jnp.exp(-g)) * u * w).astype(BF).reshape(4, 4, 16, 768)

    def down(p, s):
        k = ORDER[p][2]
        q = coord(k, s)
        index = plane_index(k, q)
        cs = slice(OSTART[p], OSTART[p] + 2 * OWIDTH[p])
        r = jnp.dot(A[index].reshape(256, 768), WD[:, cs], preferred_element_type=F32)
        X[index + (slice(None), cs)] = r.astype(BF).reshape(4, 4, 16, 2 * OWIDTH[p])

        start(
            copy(
                ("rs", p, s),
                X.at[index + (slice(None), ocols(p, 1 - c))],
                V.at[index + (slice(None), vcols(p))],
                sibling,
            )
        )

    def row_index(axis, q, i):
        rest = [a for a in range(3) if a != axis]
        idx = [None] * 3
        idx[axis] = q
        idx[rest[0]] = i
        idx[rest[1]] = slice(None)
        return tuple(idx)

    def paired(p, s):
        k = ORDER[p][2]
        q = coord(k, s)
        landed(("rs", p, s), V.at[plane_index(k, q) + (slice(None), vcols(p))])

        @pl.loop(0, 4)
        def _(i):
            at = row_index(k, q, i)
            o = at + (slice(None), ocols(p, c))
            X[o] = (X[o].astype(F32) + V[at + (slice(None), vcols(p))].astype(F32)).astype(BF)

    def oline(p, b_step, k_step):
        return line_at(p, b_step, k_step) + (ocols(p, c),)

    def send_far(p):
        for s, n in ((1, 1), (-1, 3), (1, 2), (-1, 0)):
            start(
                copy(
                    ("ra", p, s, n), X.at[oline(p, n, 2)], RA.at[n, :, :, vcols(p)],
                    device(ORDER[p][2], s),
                )
            )

    def send_near(p, s, n):
        start(
            copy(
                ("rf", p, s, n), X.at[oline(p, n, s)],
                RF.at[0 if s == 1 else 1, n, :, :, vcols(p)], device(ORDER[p][2], s),
            )
        )

    def relay_back(p, s, n):
        landed(("ra", p, s, n), RA.at[n, :, :, vcols(p)])
        o = oline(p, n, s)
        X[o] = (X[o].astype(F32) + RA[n, :, :, vcols(p)].astype(F32)).astype(BF)
        send_near(p, s, n)

    def ring_total(p, n):
        for slot, s in ((0, 1), (1, -1)):
            landed(("rf", p, s, n), RF.at[slot, n, :, :, vcols(p)])
        return (
            X[oline(p, n, 0)].astype(F32)
            + RF[0, n, :, :, vcols(p)].astype(F32)
            + RF[1, n, :, :, vcols(p)].astype(F32)
        )

    def pass_line(p, n):
        X[oline(p, n, 0)] = ring_total(p, n).astype(BF)
        start(
            copy(
                ("r2", p, n), X.at[oline(p, n, 0)], R2.at[n - 1, :, :, vcols(p)],
                device(ORDER[p][1], n),
            )
        )

    def own_line(p):
        X[oline(p, 0, 0)] = ring_total(p, 0).astype(BF)

    def gather_lines(p):
        a = ORDER[p][0]
        for n in range(3):
            landed(("r2", p, n + 1), R2.at[n, :, :, vcols(p)])
        o = oline(p, 0, 0)
        total = X[o].astype(F32)
        for n in range(3):
            total = total + R2[n, :, :, vcols(p)].astype(F32)
        X[o] = total.astype(BF)
        for n, s in enumerate(STEPS):
            fixed = list(m)
            fixed[a] = coord(a, s)
            start(
                copy(
                    ("r3", p, s), X.at[fixed[0], fixed[1], fixed[2], :, ocols(p, c)],
                    R3.at[n, :, vcols(p)], device(a, s),
                )
            )

    def gather_blocks(p):
        for n, s in enumerate(STEPS):
            landed(("r3", p, s), R3.at[n, :, vcols(p)])
        total = X[m[0], m[1], m[2], :, ocols(p, c)].astype(F32)
        for n in range(3):
            total = total + R3[n, :, vcols(p)].astype(F32)
        FB[:, vcols(p)] = total
        start(
            copy(
                ("r4", p), FB.at[pl.ds(pl.multiple_of(8 * (1 - c), 8), 8), vcols(p)],
                OB.at[:, ocols(p, c)], sibling,
            )
        )
        OB[:, ocols(p, c)] = FB[pl.ds(pl.multiple_of(8 * c, 8), 8), vcols(p)]

    for p in range(3):
        down(p, 2)
    for p in range(3):
        down(p, 1)
        paired(p, 2)
        send_far(p)
    for p in range(3):
        down(p, -1)
        paired(p, 1)
        send_near(p, 1, 3)
    for p in range(3):
        down(p, 0)
        paired(p, -1)
        send_near(p, -1, 1)
        send_near(p, -1, 2)
    for p in range(3):
        paired(p, 0)
    for p in range(3):
        relay_back(p, 1, 1)
        relay_back(p, -1, 3)
    for p in range(3):
        relay_back(p, 1, 2)
        relay_back(p, -1, 0)
        send_near(p, 1, 0)
    for n in (1, 2, 3):
        for p in range(3):
            pass_line(p, n)
    for p in range(3):
        own_line(p)
    for p in range(3):
        gather_lines(p)
    for p in range(3):
        gather_blocks(p)
    for p in range(3):
        landed(("r4", p), OB.at[:, ocols(p, 1 - c)])
    out_ref[...] = OB[...]
    for cp in sends:
        cp.wait_send()


def local(stream_in, norm_gain, expert_ids, route_weights, w_gate, w_up, w_down):
    hidden, features = w_gate.shape[0] * w_gate.shape[1], w_gate.shape[2]
    vmem = pl.BlockSpec(memory_space=pltpu.VMEM)
    hbm = pl.BlockSpec(memory_space=pl.ANY)
    return pl.pallas_call(
        functools.partial(body, table={}),
        name="moe",
        out_shape=jax.ShapeDtypeStruct((8, 4096), F32),
        in_specs=[vmem, vmem, vmem, vmem, hbm, hbm, hbm],
        out_specs=vmem,
        scratch_shapes=[
            pltpu.VMEM((4, 4, 4, 16, XW), BF),
            pltpu.VMEM((8, XW), BF),
            pltpu.VMEM((4, 2, 8, XW), BF),
            pltpu.VMEM((768, 4096), BF),
            pltpu.VMEM((768, 4096), BF),
            pltpu.VMEM((768, 4096), BF),
            pltpu.VMEM((4, 4, 4, 16, 768), F32),
            pltpu.VMEM((4, 4, 4, 16, 768), F32),
            pltpu.VMEM((4, 4, 4, 16, 768), BF),
            pltpu.VMEM((4, 4, 4, 16, 2048), BF),
            pltpu.VMEM((4, 4, 16, 2048), BF),
            pltpu.VMEM((2, 4, 4, 16, 2048), BF),
            pltpu.VMEM((3, 4, 16, 2048), BF),
            pltpu.VMEM((3, 16, 2048), BF),
            pltpu.VMEM((16, 2048), F32),
            pltpu.VMEM((8, 4096), F32),
            pltpu.VMEM((128, 768), BF),
            pltpu.SemaphoreType.DMA((224,)),
            pltpu.SemaphoreType.DMA((224,)),
            pltpu.SemaphoreType.DMA((3,)),
        ],
        compiler_params=pltpu.CompilerParams(
            collective_id=0, has_side_effects=True, vmem_limit_bytes=60 << 20
        ),
    )(
        stream_in,
        norm_gain,
        expert_ids,
        route_weights,
        w_gate.reshape(hidden, features),
        w_up.reshape(hidden, features),
        w_down.reshape(hidden, features),
    )


def solution(mesh):
    return jax.shard_map(
        local,
        mesh=mesh,
        in_specs=(
            P(("attn", "expert"), None),
            P(),
            P(("attn", "expert"), None),
            P(("attn", "expert"), None),
            P("expert", "attn", None),
            P("expert", "attn", None),
            P("expert", "attn", None),
        ),
        out_specs=P(("attn", "expert"), None),
        check_vma=False,
    )
```

```python
import functools
import jax
import jax.numpy as jnp
from jax import lax
from jax.experimental import pallas as pl
from jax.experimental.pallas import tpu as pltpu
from jax.sharding import PartitionSpec as P

BF = jnp.bfloat16
F32 = jnp.float32
MESH = pl.DeviceIdType.MESH
NT = (((1,), (1,)), ((), ()))

ORDER = ((0, 1, 2), (1, 2, 0), (2, 0, 1))
XW = 4352
HI, LO = 2816, 4224
GSTART, GWIDTH = (0, 1536, 2816), (768, 640, 768)
XK = ((0, 1536), (1536, 1280), (2944, 1280))
WK = ((0, 1536), (1536, 1280), (2816, 1280))
OSTART, OWIDTH, VSTART = (0, 1536, 2816), (768, 640, 640), (0, 768, 1408)
STEPS = (1, -1, 2)


def body(
    x_hbm, gain_hbm, ids_hbm, rw_hbm, wg_hbm, wu_hbm, wd_hbm, out_ref,
    x_ref, gain_ref, ids_ref, rw_ref,
    X, XB, XS, WG, WU, WD, G, U, A, V, RA, RF, R2, R3, SB, E, ss, rs, wsem, *, table,
):
    attn, expert = lax.axis_index("attn"), lax.axis_index("expert")
    m = (expert // 4, expert % 4, attn // 2)
    c = attn % 2

    def device(axis, step):
        n = [m[0], m[1], m[2]]
        n[axis] = (n[axis] + step + 4) % 4
        return (2 * n[2] + c, 4 * n[0] + n[1])

    sibling = (2 * m[2] + 1 - c, expert)

    def coord(axis, step):
        return (m[axis] + step + 4) % 4

    def copy(key, src, dst, dev):
        number = table.setdefault(key, len(table))
        return pltpu.make_async_remote_copy(
            src_ref=src, dst_ref=dst, send_sem=ss.at[number], recv_sem=rs.at[number],
            device_id=dev, device_id_type=MESH,
        )

    def plane_index(axis, q):
        idx = [slice(None)] * 3
        idx[axis] = q
        return tuple(idx)

    def line_at(p, b_step, k_step):
        a, b, k = ORDER[p]
        idx = [slice(None)] * 3
        idx[b], idx[k] = coord(b, b_step), coord(k, k_step)
        return tuple(idx) + (slice(None),)

    def gcols(p, core):
        return pl.ds(pl.multiple_of(GSTART[p] + core * GWIDTH[p], 128), GWIDTH[p])

    def ocols(p, core):
        return pl.ds(pl.multiple_of(OSTART[p] + core * OWIDTH[p], 128), OWIDTH[p])

    def vcols(p):
        return pl.ds(VSTART[p], OWIDTH[p])

    small = [
        pltpu.make_async_copy(h, v, wsem.at[3 + i])
        for i, (h, v) in enumerate(
            ((x_hbm, x_ref), (gain_hbm, gain_ref), (ids_hbm, ids_ref), (rw_hbm, rw_ref))
        )
    ]
    for load in small:
        load.start()
    loads = [
        pltpu.make_async_copy(h, v, wsem.at[i])
        for i, (h, v) in enumerate(((wg_hbm, WG), (wu_hbm, WU), (wd_hbm, WD)))
    ]
    for load in loads:
        load.start()

    barrier = pltpu.get_barrier_semaphore()
    def across(dev):
        return (dev[0] + 1 - 2 * c, dev[1])

    partners = [sibling]
    for a in range(3):
        for s in STEPS:
            partners += [device(a, s), across(device(a, s))]
    for dev in partners:
        pl.semaphore_signal(barrier, inc=1, device_id=dev, device_id_type=MESH)

    for load in small:
        load.wait()

    lane = lax.broadcasted_iota(jnp.int32, (8, 128), 1)
    spread = jnp.zeros((8, 128), F32)
    for k in range(8):
        spread = spread + jnp.where(ids_ref[:, k : k + 1] == lane, rw_ref[:, k : k + 1], 0.0)
    high = spread.astype(BF)
    low = (spread - high.astype(F32)).astype(BF)
    stream = x_ref[...].astype(F32)
    inverse = lax.rsqrt(jnp.sum(stream * stream, axis=-1, keepdims=True) * (1.0 / 4096) + 1e-06)
    normed = (stream * inverse * gain_ref[...].astype(F32).reshape(1, 4096)).astype(BF)
    XB[:, 0:HI] = normed[:, 0:HI]
    XB[:, HI : HI + 128] = high
    XB[:, HI + 128 : LO] = normed[:, HI:4096]
    XB[:, LO:XW] = low

    er = lax.broadcasted_iota(jnp.int32, (128, 768), 0)
    ec = lax.broadcasted_iota(jnp.int32, (128, 768), 1)
    held = er - 4 * expert
    E[...] = jnp.where((ec >= held * 192) & (ec < held * 192 + 192), 1.0, 0.0).astype(BF)

    @pl.loop(0, 16)
    def _(i):
        G[i // 4, i % 4] = jnp.zeros((4, 16, 768), F32)
        U[i // 4, i % 4] = jnp.zeros((4, 16, 768), F32)

    pl.semaphore_wait(barrier, len(partners))
    sends = []

    def start(cp):
        cp.start()
        sends.append(cp)

    def landed(key, ref):
        copy(key, ref, ref, sibling).wait_recv()

    def gline(p, b_step, k_step):
        return X.at[line_at(p, b_step, k_step) + (gcols(p, c),)]

    def send_line(p, s, b_step):
        start(
            copy(
                ("g3", p, s, b_step), gline(p, b_step, 0), gline(p, b_step, 0),
                device(ORDER[p][2], s),
            )
        )

    def stage1(p):
        a = ORDER[p][0]
        mine, other = gcols(p, c), gcols(p, 1 - c)
        start(copy(("g0", p), XB.at[:, other], XS.at[0, c, :, other], sibling))
        for i, s in enumerate(STEPS):
            dev = device(a, s)
            start(copy(("g1", p, s, 0), XB.at[:, mine], XS.at[i + 1, c, :, mine], dev))
            start(copy(("g1", p, s, 1), XB.at[:, other], XS.at[i + 1, c, :, other], across(dev)))

    def gblock(p, b_step, a_step):
        a, b, _ = ORDER[p]
        n = list(m)
        n[a], n[b] = coord(a, a_step), coord(b, b_step)
        return (n[0], n[1], n[2], slice(None), gcols(p, c))

    def stage2(p, i):
        b = ORDER[p][1]
        mine = gcols(p, c)
        if i == 0:
            XS[0, c, :, mine] = XB[:, mine]
            landed(("g0", p), XS.at[0, 1 - c, :, mine])
            a_step = 0
        else:
            a_step = -STEPS[i - 1]
            landed(("g1", p, STEPS[i - 1], 0), XS.at[i, c, :, mine])
            landed(("g1", p, STEPS[i - 1], 1), XS.at[i, 1 - c, :, mine])
        rows = jnp.concatenate(
            [XS[i, 0, :, mine].astype(F32), XS[i, 1, :, mine].astype(F32)], axis=0
        )
        X[gblock(p, 0, a_step)] = rows.astype(BF)
        ref = X.at[gblock(p, 0, a_step)]
        for s in STEPS:
            start(copy(("g2", p, s, i), ref, ref, device(b, s)))

    def xplane(p, q, core):
        return X.at[plane_index(ORDER[p][2], q) + (slice(None), gcols(p, core))]

    def stage3(p):
        k = ORDER[p][2]
        for i in range(4):
            for s in STEPS:
                a_step = 0 if i == 0 else -STEPS[i - 1]
                landed(("g2", p, s, i), X.at[gblock(p, -s, a_step)])
        for n in (1, 2, 3):
            send_line(p, 1, n)
            send_line(p, -1, 4 - n)
        ref = xplane(p, m[k], c)
        start(copy(("gs", p, 0), ref, ref, sibling))

    def relay(p, s, b_step):
        ref = gline(p, b_step, -s)
        landed(("g3", p, s, b_step), ref)
        start(copy(("gr", p, s, b_step), ref, ref, device(ORDER[p][2], s)))
        start(copy(("gl", p, s, b_step), ref, ref, sibling))

    def share(p, s, b_step):
        ref = gline(p, b_step, -s)
        landed(("g3", p, s, b_step), ref)
        start(copy(("gl", p, s, b_step), ref, ref, sibling))

    def share_far(p):
        for s, n in ((1, 0), (-1, 3), (1, 1), (-1, 2)):
            ref = gline(p, n, 2)
            landed(("gr", p, s, n), ref)
            start(copy(("gl", p, 2, n), ref, ref, sibling))

    def unit(p, s):
        k = ORDER[p][2]
        q = coord(k, -s)
        if s == 0:
            landed(("gs", p, 0), xplane(p, q, 1 - c))
        else:
            for n in range(4):
                landed(("gl", p, s, n), X.at[line_at(p, n, -s) + (gcols(p, 1 - c),)])
        index = plane_index(k, q)
        x0, xn = XK[p]
        w0, wn = WK[p]

        xs = X[index + (slice(None), slice(x0, x0 + xn))].reshape(256, xn)
        for w, acc in ((WG, G), (WU, U)):
            r = lax.dot_general(xs, w[:, w0 : w0 + wn], NT, preferred_element_type=F32)
            acc[index] += r.reshape(4, 4, 16, 768)

    for p in range(3):
        stage1(p)

    for i in range(4):
        for p in range(3):
            stage2(p, i)
    for p in range(3):
        send_line(p, 1, 0)
        send_line(p, -1, 0)
    for p in range(3):
        stage3(p)
    for p in range(3):
        relay(p, 1, 0)
        share(p, -1, 0)
    loads[0].wait()
    loads[1].wait()
    for p in range(3):
        unit(p, 0)
    for p in range(3):
        relay(p, -1, 3)
        relay(p, 1, 1)
    for p in range(3):
        relay(p, -1, 2)
        share(p, 1, 2)
    for p in range(3):
        share(p, 1, 3)
        share(p, -1, 1)
    for p in range(3):
        unit(p, 1)
    for p in range(3):
        share_far(p)
    for p in range(3):
        unit(p, -1)
    for p in range(3):
        unit(p, 2)
    loads[2].wait()
    for cp in sends:
        cp.wait_send()
    sends.clear()

    @pl.loop(0, 4)
    def _(i):
        g = G[i].reshape(256, 768)
        u = U[i].reshape(256, 768)
        hi = X[i, :, :, :, HI : HI + 128].reshape(256, 128)
        lo = X[i, :, :, :, LO:XW].reshape(256, 128)
        w = jnp.dot(hi, E[...], preferred_element_type=F32) + jnp.dot(
            lo, E[...], preferred_element_type=F32
        )
        A[i] = (g / (1.0 + jnp.exp(-g)) * u * w).astype(BF).reshape(4, 4, 16, 768)

    def down(p, s):
        k = ORDER[p][2]
        q = coord(k, s)
        index = plane_index(k, q)
        cs = slice(OSTART[p], OSTART[p] + 2 * OWIDTH[p])
        r = jnp.dot(A[index].reshape(256, 768), WD[:, cs], preferred_element_type=F32)
        X[index + (slice(None), cs)] = r.astype(BF).reshape(4, 4, 16, 2 * OWIDTH[p])

        start(
            copy(
                ("rs", p, s),
                X.at[index + (slice(None), ocols(p, 1 - c))],
                V.at[index + (slice(None), vcols(p))],
                sibling,
            )
        )

    def row_index(axis, q, i):
        rest = [a for a in range(3) if a != axis]
        idx = [None] * 3
        idx[axis] = q
        idx[rest[0]] = i
        idx[rest[1]] = slice(None)
        return tuple(idx)

    def paired(p, s):
        k = ORDER[p][2]
        q = coord(k, s)
        landed(("rs", p, s), V.at[plane_index(k, q) + (slice(None), vcols(p))])

        @pl.loop(0, 4)
        def _(i):
            at = row_index(k, q, i)
            o = at + (slice(None), ocols(p, c))
            X[o] = (X[o].astype(F32) + V[at + (slice(None), vcols(p))].astype(F32)).astype(BF)

    def oline(p, b_step, k_step):
        return line_at(p, b_step, k_step) + (ocols(p, c),)

    def send_far(p):
        for s, n in ((1, 1), (-1, 3), (1, 2), (-1, 0)):
            start(
                copy(
                    ("ra", p, s, n), X.at[oline(p, n, 2)], RA.at[n, :, :, vcols(p)],
                    device(ORDER[p][2], s),
                )
            )

    def send_near(p, s, n):
        start(
            copy(
                ("rf", p, s, n), X.at[oline(p, n, s)],
                RF.at[0 if s == 1 else 1, n, :, :, vcols(p)], device(ORDER[p][2], s),
            )
        )

    def relay_back(p, s, n):
        landed(("ra", p, s, n), RA.at[n, :, :, vcols(p)])
        o = oline(p, n, s)
        X[o] = (X[o].astype(F32) + RA[n, :, :, vcols(p)].astype(F32)).astype(BF)
        send_near(p, s, n)

    def ring_total(p, n):
        for slot, s in ((0, 1), (1, -1)):
            landed(("rf", p, s, n), RF.at[slot, n, :, :, vcols(p)])
        return (
            X[oline(p, n, 0)].astype(F32)
            + RF[0, n, :, :, vcols(p)].astype(F32)
            + RF[1, n, :, :, vcols(p)].astype(F32)
        )

    def pass_line(p, n):
        X[oline(p, n, 0)] = ring_total(p, n).astype(BF)
        start(
            copy(
                ("r2", p, n), X.at[oline(p, n, 0)], R2.at[n - 1, :, :, vcols(p)],
                device(ORDER[p][1], n),
            )
        )

    def own_line(p):
        X[oline(p, 0, 0)] = ring_total(p, 0).astype(BF)

    def gather_lines(p):
        a = ORDER[p][0]
        for n in range(3):
            landed(("r2", p, n + 1), R2.at[n, :, :, vcols(p)])
        o = oline(p, 0, 0)
        total = X[o].astype(F32)
        for n in range(3):
            total = total + R2[n, :, :, vcols(p)].astype(F32)
        SB[:, 0, :, vcols(p)] = total[:, 0:8].astype(BF)
        SB[:, 1, :, vcols(p)] = total[:, 8:16].astype(BF)
        for n, s in enumerate(STEPS):
            dev, at = device(a, s), coord(a, s)
            for kind, core, to in ((0, c, dev), (1, 1 - c, across(dev))):
                start(
                    copy(
                        ("r3", p, s, kind), SB.at[at, core, :, vcols(p)],
                        R3.at[n + 1, kind, :, vcols(p)], to,
                    )
                )
        start(
            copy(("r4", p), SB.at[m[a], 1 - c, :, vcols(p)], R3.at[0, 1, :, vcols(p)], sibling)
        )

    def gather_blocks(p):
        landed(("r4", p), R3.at[0, 1, :, vcols(p)])
        for n, s in enumerate(STEPS):
            for kind in range(2):
                landed(("r3", p, s, kind), R3.at[n + 1, kind, :, vcols(p)])
        mine = SB[m[ORDER[p][0]], c, :, vcols(p)].astype(F32)
        other = R3[0, 1, :, vcols(p)].astype(F32)
        for n in range(1, 4):
            mine = mine + R3[n, 0, :, vcols(p)].astype(F32)
            other = other + R3[n, 1, :, vcols(p)].astype(F32)
        out_ref[:, ocols(p, c)] = mine
        out_ref[:, ocols(p, 1 - c)] = other

    for p in range(3):
        down(p, 2)
    for p in range(3):
        down(p, 1)
        paired(p, 2)
        send_far(p)
    for p in range(3):
        down(p, -1)
        paired(p, 1)
        send_near(p, 1, 3)
    for p in range(3):
        down(p, 0)
        paired(p, -1)
        send_near(p, -1, 1)
        send_near(p, -1, 2)
    for p in range(3):
        paired(p, 0)
    for p in range(3):
        relay_back(p, 1, 1)
        relay_back(p, -1, 3)
    for p in range(3):
        relay_back(p, 1, 2)
        relay_back(p, -1, 0)
        send_near(p, 1, 0)
    for n in (1, 2, 3):
        for p in range(3):
            pass_line(p, n)
    for p in range(3):
        own_line(p)
    for p in range(3):
        gather_lines(p)
    for p in range(3):
        gather_blocks(p)
    for cp in sends:
        cp.wait_send()


def local(stream_in, norm_gain, expert_ids, route_weights, w_gate, w_up, w_down):
    hidden, features = w_gate.shape[0] * w_gate.shape[1], w_gate.shape[2]
    vmem = pl.BlockSpec(memory_space=pltpu.VMEM)
    hbm = pl.BlockSpec(memory_space=pl.ANY)
    return pl.pallas_call(
        functools.partial(body, table={}),
        name="moe",
        out_shape=jax.ShapeDtypeStruct((8, 4096), F32),
        in_specs=[hbm] * 7,
        out_specs=vmem,
        scratch_shapes=[
            pltpu.VMEM((8, 4096), BF),
            pltpu.VMEM((4096,), BF),
            pltpu.VMEM((8, 8), jnp.int32),
            pltpu.VMEM((8, 8), F32),
            pltpu.VMEM((4, 4, 4, 16, XW), BF),
            pltpu.VMEM((8, XW), BF),
            pltpu.VMEM((4, 2, 8, XW), BF),
            pltpu.VMEM((768, 4096), BF),
            pltpu.VMEM((768, 4096), BF),
            pltpu.VMEM((768, 4096), BF),
            pltpu.VMEM((4, 4, 4, 16, 768), F32),
            pltpu.VMEM((4, 4, 4, 16, 768), F32),
            pltpu.VMEM((4, 4, 4, 16, 768), BF),
            pltpu.VMEM((4, 4, 4, 16, 2048), BF),
            pltpu.VMEM((4, 4, 16, 2048), BF),
            pltpu.VMEM((2, 4, 4, 16, 2048), BF),
            pltpu.VMEM((3, 4, 16, 2048), BF),
            pltpu.VMEM((4, 2, 8, 2048), BF),
            pltpu.VMEM((4, 2, 8, 2048), BF),
            pltpu.VMEM((128, 768), BF),
            pltpu.SemaphoreType.DMA((224,)),
            pltpu.SemaphoreType.DMA((224,)),
            pltpu.SemaphoreType.DMA((7,)),
        ],
        compiler_params=pltpu.CompilerParams(
            collective_id=0, has_side_effects=True, vmem_limit_bytes=60 << 20
        ),
    )(
        stream_in,
        norm_gain,
        expert_ids,
        route_weights,
        w_gate.reshape(hidden, features),
        w_up.reshape(hidden, features),
        w_down.reshape(hidden, features),
    )


def solution(mesh):
    return jax.shard_map(
        local,
        mesh=mesh,
        in_specs=(
            P(("attn", "expert"), None),
            P(),
            P(("attn", "expert"), None),
            P(("attn", "expert"), None),
            P("expert", "attn", None),
            P("expert", "attn", None),
            P("expert", "attn", None),
        ),
        out_specs=P(("attn", "expert"), None),
        check_vma=False,
    )
```

```python
import functools
import jax
import jax.numpy as jnp
from jax import lax
from jax.experimental import pallas as pl
from jax.experimental.pallas import tpu as pltpu
from jax.sharding import PartitionSpec as P

BF = jnp.bfloat16
F32 = jnp.float32
MESH = pl.DeviceIdType.MESH
NT = (((1,), (1,)), ((), ()))

ORDER = ((0, 1, 2), (1, 2, 0), (2, 0, 1))
XW = 4352
HI, LO = 2816, 4224
GSTART, GWIDTH = (0, 1536, 2816), (768, 640, 768)
XK = ((0, 1536), (1536, 1280), (2944, 1280))
WK = ((0, 1536), (1536, 1280), (2816, 1280))
OSTART, OWIDTH, VSTART = (0, 1536, 2816), (768, 640, 640), (0, 768, 1408)
STEPS = (1, -1, 2)


def body(
    x_hbm, gain_hbm, ids_hbm, rw_hbm, wg_hbm, wu_hbm, wd_hbm, out_ref,
    x_ref, gain_ref, ids_ref, rw_ref,
    X, XB, XS, WG, WU, WD, G, U, A, V, RA, RF, R2, R3, SB, E, ss, rs, wsem, *, table,
):
    attn, expert = lax.axis_index("attn"), lax.axis_index("expert")
    m = (expert // 4, expert % 4, attn // 2)
    c = attn % 2

    def device(axis, step):
        n = [m[0], m[1], m[2]]
        n[axis] = (n[axis] + step + 4) % 4
        return (2 * n[2] + c, 4 * n[0] + n[1])

    sibling = (2 * m[2] + 1 - c, expert)

    def coord(axis, step):
        return (m[axis] + step + 4) % 4

    def copy(key, src, dst, dev):
        number = table.setdefault(key, len(table))
        return pltpu.make_async_remote_copy(
            src_ref=src, dst_ref=dst, send_sem=ss.at[number], recv_sem=rs.at[number],
            device_id=dev, device_id_type=MESH,
        )

    def plane_index(axis, q):
        idx = [slice(None)] * 3
        idx[axis] = q
        return tuple(idx)

    def line_at(p, b_step, k_step):
        a, b, k = ORDER[p]
        idx = [slice(None)] * 3
        idx[b], idx[k] = coord(b, b_step), coord(k, k_step)
        return tuple(idx) + (slice(None),)

    def gcols(p, core):
        return pl.ds(pl.multiple_of(GSTART[p] + core * GWIDTH[p], 128), GWIDTH[p])

    def ocols(p, core):
        return pl.ds(pl.multiple_of(OSTART[p] + core * OWIDTH[p], 128), OWIDTH[p])

    def vcols(p):
        return pl.ds(VSTART[p], OWIDTH[p])

    small = [
        pltpu.make_async_copy(h, v, wsem.at[3 + i])
        for i, (h, v) in enumerate(
            ((x_hbm, x_ref), (gain_hbm, gain_ref), (ids_hbm, ids_ref), (rw_hbm, rw_ref))
        )
    ]
    for load in small:
        load.start()
    loads = [
        pltpu.make_async_copy(h, v, wsem.at[i])
        for i, (h, v) in enumerate(((wg_hbm, WG), (wu_hbm, WU), (wd_hbm, WD)))
    ]
    for load in loads:
        load.start()

    barrier = pltpu.get_barrier_semaphore()
    def across(dev):
        return (dev[0] + 1 - 2 * c, dev[1])

    partners = [sibling]
    for a in range(3):
        for s in STEPS:
            partners += [device(a, s), across(device(a, s))]
    for dev in partners:
        pl.semaphore_signal(barrier, inc=1, device_id=dev, device_id_type=MESH)

    for load in small:
        load.wait()

    lane = lax.broadcasted_iota(jnp.int32, (8, 128), 1)
    spread = jnp.zeros((8, 128), F32)
    for k in range(8):
        spread = spread + jnp.where(ids_ref[:, k : k + 1] == lane, rw_ref[:, k : k + 1], 0.0)
    high = spread.astype(BF)
    low = (spread - high.astype(F32)).astype(BF)
    stream = x_ref[...].astype(F32)
    inverse = lax.rsqrt(jnp.sum(stream * stream, axis=-1, keepdims=True) * (1.0 / 4096) + 1e-06)
    normed = (stream * inverse * gain_ref[...].astype(F32).reshape(1, 4096)).astype(BF)
    XB[:, 0:HI] = normed[:, 0:HI]
    XB[:, HI : HI + 128] = high
    XB[:, HI + 128 : LO] = normed[:, HI:4096]
    XB[:, LO:XW] = low

    er = lax.broadcasted_iota(jnp.int32, (128, 768), 0)
    ec = lax.broadcasted_iota(jnp.int32, (128, 768), 1)
    held = er - 4 * expert
    E[...] = jnp.where((ec >= held * 192) & (ec < held * 192 + 192), 1.0, 0.0).astype(BF)

    @pl.loop(0, 16)
    def _(i):
        G[i // 4, i % 4] = jnp.zeros((4, 16, 768), F32)
        U[i // 4, i % 4] = jnp.zeros((4, 16, 768), F32)

    pl.semaphore_wait(barrier, len(partners))
    sends = []

    def start(cp):
        cp.start()
        sends.append(cp)

    def drain(count=None):
        for cp in sends[:count]:
            cp.wait_send()
        del sends[:count]

    def landed(key, ref):
        copy(key, ref, ref, sibling).wait_recv()

    def gline(p, b_step, k_step):
        return X.at[line_at(p, b_step, k_step) + (gcols(p, c),)]

    def send_line(p, s, b_step):
        start(
            copy(
                ("g3", p, s, b_step), gline(p, b_step, 0), gline(p, b_step, 0),
                device(ORDER[p][2], s),
            )
        )

    def stage1(p):
        a = ORDER[p][0]
        mine, other = gcols(p, c), gcols(p, 1 - c)
        start(copy(("g0", p), XB.at[:, other], XS.at[0, c, :, other], sibling))
        for i, s in enumerate(STEPS):
            dev = device(a, s)
            start(copy(("g1", p, s, 0), XB.at[:, mine], XS.at[i + 1, c, :, mine], dev))
            start(copy(("g1", p, s, 1), XB.at[:, other], XS.at[i + 1, c, :, other], across(dev)))

    def gblock(p, b_step, a_step):
        a, b, _ = ORDER[p]
        n = list(m)
        n[a], n[b] = coord(a, a_step), coord(b, b_step)
        return (n[0], n[1], n[2], slice(None), gcols(p, c))

    def stage2(p, i):
        b = ORDER[p][1]
        mine = gcols(p, c)
        if i == 0:
            XS[0, c, :, mine] = XB[:, mine]
            landed(("g0", p), XS.at[0, 1 - c, :, mine])
            a_step = 0
        else:
            a_step = -STEPS[i - 1]
            landed(("g1", p, STEPS[i - 1], 0), XS.at[i, c, :, mine])
            landed(("g1", p, STEPS[i - 1], 1), XS.at[i, 1 - c, :, mine])
        rows = jnp.concatenate(
            [XS[i, 0, :, mine].astype(F32), XS[i, 1, :, mine].astype(F32)], axis=0
        )
        X[gblock(p, 0, a_step)] = rows.astype(BF)
        ref = X.at[gblock(p, 0, a_step)]
        for s in STEPS:
            start(copy(("g2", p, s, i), ref, ref, device(b, s)))

    def xplane(p, q, core):
        return X.at[plane_index(ORDER[p][2], q) + (slice(None), gcols(p, core))]

    def stage3(p):
        k = ORDER[p][2]
        for i in range(4):
            for s in STEPS:
                a_step = 0 if i == 0 else -STEPS[i - 1]
                landed(("g2", p, s, i), X.at[gblock(p, -s, a_step)])
        for n in (1, 2, 3):
            send_line(p, 1, n)
            send_line(p, -1, 4 - n)
        ref = xplane(p, m[k], c)
        start(copy(("gs", p, 0), ref, ref, sibling))

    def relay(p, s, b_step):
        ref = gline(p, b_step, -s)
        landed(("g3", p, s, b_step), ref)
        start(copy(("gr", p, s, b_step), ref, ref, device(ORDER[p][2], s)))
        start(copy(("gl", p, s, b_step), ref, ref, sibling))

    def share(p, s, b_step):
        ref = gline(p, b_step, -s)
        landed(("g3", p, s, b_step), ref)
        start(copy(("gl", p, s, b_step), ref, ref, sibling))

    def share_far(p):
        for s, n in ((1, 0), (-1, 3), (1, 1), (-1, 2)):
            ref = gline(p, n, 2)
            landed(("gr", p, s, n), ref)
            start(copy(("gl", p, 2, n), ref, ref, sibling))

    def unit(p, s):
        k = ORDER[p][2]
        q = coord(k, -s)
        if s == 0:
            landed(("gs", p, 0), xplane(p, q, 1 - c))
        else:
            for n in range(4):
                landed(("gl", p, s, n), X.at[line_at(p, n, -s) + (gcols(p, 1 - c),)])
        index = plane_index(k, q)
        x0, xn = XK[p]
        w0, wn = WK[p]

        xs = X[index + (slice(None), slice(x0, x0 + xn))].reshape(256, xn)
        for w, acc in ((WG, G), (WU, U)):
            r = lax.dot_general(xs, w[:, w0 : w0 + wn], NT, preferred_element_type=F32)
            acc[index] += r.reshape(4, 4, 16, 768)

    for p in range(3):
        stage1(p)

    for i in range(4):
        for p in range(3):
            stage2(p, i)
    for p in range(3):
        send_line(p, 1, 0)
        send_line(p, -1, 0)
    early = len(sends)
    for p in range(3):
        stage3(p)
    for p in range(3):
        relay(p, 1, 0)
        share(p, -1, 0)
    loads[0].wait()
    loads[1].wait()
    drain(early)
    for p in range(3):
        unit(p, 0)
    for p in range(3):
        relay(p, -1, 3)
        relay(p, 1, 1)
    for p in range(3):
        relay(p, -1, 2)
        share(p, 1, 2)
    for p in range(3):
        share(p, 1, 3)
        share(p, -1, 1)
    for p in range(3):
        unit(p, 1)
    drain()
    for p in range(3):
        share_far(p)
    for p in range(3):
        unit(p, -1)
    for p in range(3):
        unit(p, 2)
    loads[2].wait()
    drain()

    @pl.loop(0, 4)
    def _(i):
        g = G[i].reshape(256, 768)
        u = U[i].reshape(256, 768)
        hi = X[i, :, :, :, HI : HI + 128].reshape(256, 128)
        lo = X[i, :, :, :, LO:XW].reshape(256, 128)
        w = jnp.dot(hi, E[...], preferred_element_type=F32) + jnp.dot(
            lo, E[...], preferred_element_type=F32
        )
        A[i] = (g / (1.0 + jnp.exp(-g)) * u * w).astype(BF).reshape(4, 4, 16, 768)

    def down(p, s):
        k = ORDER[p][2]
        q = coord(k, s)
        index = plane_index(k, q)
        cs = slice(OSTART[p], OSTART[p] + 2 * OWIDTH[p])
        r = jnp.dot(A[index].reshape(256, 768), WD[:, cs], preferred_element_type=F32)
        X[index + (slice(None), cs)] = r.astype(BF).reshape(4, 4, 16, 2 * OWIDTH[p])

        start(
            copy(
                ("rs", p, s),
                X.at[index + (slice(None), ocols(p, 1 - c))],
                V.at[index + (slice(None), vcols(p))],
                sibling,
            )
        )

    def row_index(axis, q, i):
        rest = [a for a in range(3) if a != axis]
        idx = [None] * 3
        idx[axis] = q
        idx[rest[0]] = i
        idx[rest[1]] = slice(None)
        return tuple(idx)

    def paired(p, s):
        k = ORDER[p][2]
        q = coord(k, s)
        landed(("rs", p, s), V.at[plane_index(k, q) + (slice(None), vcols(p))])

        @pl.loop(0, 4)
        def _(i):
            at = row_index(k, q, i)
            o = at + (slice(None), ocols(p, c))
            X[o] = (X[o].astype(F32) + V[at + (slice(None), vcols(p))].astype(F32)).astype(BF)

    def oline(p, b_step, k_step):
        return line_at(p, b_step, k_step) + (ocols(p, c),)

    def send_far(p):
        for s, n in ((1, 1), (-1, 3), (1, 2), (-1, 0)):
            start(
                copy(
                    ("ra", p, s, n), X.at[oline(p, n, 2)], RA.at[n, :, :, vcols(p)],
                    device(ORDER[p][2], s),
                )
            )

    def send_near(p, s, n):
        start(
            copy(
                ("rf", p, s, n), X.at[oline(p, n, s)],
                RF.at[0 if s == 1 else 1, n, :, :, vcols(p)], device(ORDER[p][2], s),
            )
        )

    def relay_back(p, s, n):
        landed(("ra", p, s, n), RA.at[n, :, :, vcols(p)])
        o = oline(p, n, s)
        X[o] = (X[o].astype(F32) + RA[n, :, :, vcols(p)].astype(F32)).astype(BF)
        send_near(p, s, n)

    def ring_total(p, n):
        for slot, s in ((0, 1), (1, -1)):
            landed(("rf", p, s, n), RF.at[slot, n, :, :, vcols(p)])
        return (
            X[oline(p, n, 0)].astype(F32)
            + RF[0, n, :, :, vcols(p)].astype(F32)
            + RF[1, n, :, :, vcols(p)].astype(F32)
        )

    def pass_line(p, n):
        X[oline(p, n, 0)] = ring_total(p, n).astype(BF)
        start(
            copy(
                ("r2", p, n), X.at[oline(p, n, 0)], R2.at[n - 1, :, :, vcols(p)],
                device(ORDER[p][1], n),
            )
        )

    def own_line(p):
        X[oline(p, 0, 0)] = ring_total(p, 0).astype(BF)

    def gather_lines(p):
        a = ORDER[p][0]
        for n in range(3):
            landed(("r2", p, n + 1), R2.at[n, :, :, vcols(p)])
        o = oline(p, 0, 0)
        total = X[o].astype(F32)
        for n in range(3):
            total = total + R2[n, :, :, vcols(p)].astype(F32)
        SB[:, 0, :, vcols(p)] = total[:, 0:8].astype(BF)
        SB[:, 1, :, vcols(p)] = total[:, 8:16].astype(BF)
        for n, s in enumerate(STEPS):
            dev, at = device(a, s), coord(a, s)
            for kind, core, to in ((0, c, dev), (1, 1 - c, across(dev))):
                start(
                    copy(
                        ("r3", p, s, kind), SB.at[at, core, :, vcols(p)],
                        R3.at[n + 1, kind, :, vcols(p)], to,
                    )
                )
        start(
            copy(("r4", p), SB.at[m[a], 1 - c, :, vcols(p)], R3.at[0, 1, :, vcols(p)], sibling)
        )

    def gather_blocks(p):
        landed(("r4", p), R3.at[0, 1, :, vcols(p)])
        for n, s in enumerate(STEPS):
            for kind in range(2):
                landed(("r3", p, s, kind), R3.at[n + 1, kind, :, vcols(p)])
        mine = SB[m[ORDER[p][0]], c, :, vcols(p)].astype(F32)
        other = R3[0, 1, :, vcols(p)].astype(F32)
        for n in range(1, 4):
            mine = mine + R3[n, 0, :, vcols(p)].astype(F32)
            other = other + R3[n, 1, :, vcols(p)].astype(F32)
        out_ref[:, ocols(p, c)] = mine
        out_ref[:, ocols(p, 1 - c)] = other

    for p in range(3):
        down(p, 2)
    for p in range(3):
        down(p, 1)
        paired(p, 2)
        send_far(p)
    for p in range(3):
        down(p, -1)
        paired(p, 1)
        send_near(p, 1, 3)
    for p in range(3):
        down(p, 0)
        paired(p, -1)
        send_near(p, -1, 1)
        send_near(p, -1, 2)
    for p in range(3):
        paired(p, 0)
    for p in range(3):
        relay_back(p, 1, 1)
        relay_back(p, -1, 3)
    for p in range(3):
        relay_back(p, 1, 2)
        relay_back(p, -1, 0)
        send_near(p, 1, 0)
    for n in (1, 2, 3):
        for p in range(3):
            pass_line(p, n)
    for p in range(3):
        own_line(p)
    drain()
    for p in range(3):
        gather_lines(p)
    for p in range(3):
        gather_blocks(p)
    drain()


def local(stream_in, norm_gain, expert_ids, route_weights, w_gate, w_up, w_down):
    hidden, features = w_gate.shape[0] * w_gate.shape[1], w_gate.shape[2]
    vmem = pl.BlockSpec(memory_space=pltpu.VMEM)
    hbm = pl.BlockSpec(memory_space=pl.ANY)
    return pl.pallas_call(
        functools.partial(body, table={}),
        name="moe",
        out_shape=jax.ShapeDtypeStruct((8, 4096), F32),
        in_specs=[hbm] * 7,
        out_specs=vmem,
        scratch_shapes=[
            pltpu.VMEM((8, 4096), BF),
            pltpu.VMEM((4096,), BF),
            pltpu.VMEM((8, 8), jnp.int32),
            pltpu.VMEM((8, 8), F32),
            pltpu.VMEM((4, 4, 4, 16, XW), BF),
            pltpu.VMEM((8, XW), BF),
            pltpu.VMEM((4, 2, 8, XW), BF),
            pltpu.VMEM((768, 4096), BF),
            pltpu.VMEM((768, 4096), BF),
            pltpu.VMEM((768, 4096), BF),
            pltpu.VMEM((4, 4, 4, 16, 768), F32),
            pltpu.VMEM((4, 4, 4, 16, 768), F32),
            pltpu.VMEM((4, 4, 4, 16, 768), BF),
            pltpu.VMEM((4, 4, 4, 16, 2048), BF),
            pltpu.VMEM((4, 4, 16, 2048), BF),
            pltpu.VMEM((2, 4, 4, 16, 2048), BF),
            pltpu.VMEM((3, 4, 16, 2048), BF),
            pltpu.VMEM((4, 2, 8, 2048), BF),
            pltpu.VMEM((4, 2, 8, 2048), BF),
            pltpu.VMEM((128, 768), BF),
            pltpu.SemaphoreType.DMA((224,)),
            pltpu.SemaphoreType.DMA((224,)),
            pltpu.SemaphoreType.DMA((7,)),
        ],
        compiler_params=pltpu.CompilerParams(
            collective_id=0, has_side_effects=True, vmem_limit_bytes=60 << 20
        ),
    )(
        stream_in,
        norm_gain,
        expert_ids,
        route_weights,
        w_gate.reshape(hidden, features),
        w_up.reshape(hidden, features),
        w_down.reshape(hidden, features),
    )


def solution(mesh):
    return jax.shard_map(
        local,
        mesh=mesh,
        in_specs=(
            P(("attn", "expert"), None),
            P(),
            P(("attn", "expert"), None),
            P(("attn", "expert"), None),
            P("expert", "attn", None),
            P("expert", "attn", None),
            P("expert", "attn", None),
        ),
        out_specs=P(("attn", "expert"), None),
        check_vma=False,
    )
```

```python
import functools
import jax
import jax.numpy as jnp
from jax import lax
from jax.experimental import pallas as pl
from jax.experimental.pallas import tpu as pltpu
from jax.sharding import PartitionSpec as P

BF = jnp.bfloat16
F32 = jnp.float32
MESH = pl.DeviceIdType.MESH
NT = (((1,), (1,)), ((), ()))

ORDER = ((0, 1, 2), (1, 2, 0), (2, 0, 1))
XW = 4352
HI, LO = 2816, 4224
GSTART, GWIDTH = (0, 1536, 2816), (768, 640, 768)
XK = ((0, 1536), (1536, 1280), (2944, 1280))
WK = ((0, 1536), (1536, 1280), (2816, 1280))
OSTART, OWIDTH, VSTART = (0, 1536, 2816), (768, 640, 640), (0, 768, 1408)
STEPS = (1, -1, 2)


def body(
    x_hbm, gain_hbm, ids_hbm, rw_hbm, wg_hbm, wu_hbm, wd_hbm, out_ref,
    x_ref, gain_ref, ids_ref, rw_ref,
    X, XB, XS, WG, WU, WD, G, U, A, V, RA, RF, R2, R3, SB, E, ss, rs, wsem, *, table,
):
    attn, expert = lax.axis_index("attn"), lax.axis_index("expert")
    m = (expert // 4, expert % 4, attn // 2)
    c = attn % 2

    def device(axis, step):
        n = [m[0], m[1], m[2]]
        n[axis] = (n[axis] + step + 4) % 4
        return (2 * n[2] + c, 4 * n[0] + n[1])

    sibling = (2 * m[2] + 1 - c, expert)

    def coord(axis, step):
        return (m[axis] + step + 4) % 4

    def copy(key, src, dst, dev):
        number = table.setdefault(key, len(table))
        return pltpu.make_async_remote_copy(
            src_ref=src, dst_ref=dst, send_sem=ss.at[number], recv_sem=rs.at[number],
            device_id=dev, device_id_type=MESH,
        )

    def plane_index(axis, q):
        idx = [slice(None)] * 3
        idx[axis] = q
        return tuple(idx)

    def line_at(p, b_step, k_step):
        a, b, k = ORDER[p]
        idx = [slice(None)] * 3
        idx[b], idx[k] = coord(b, b_step), coord(k, k_step)
        return tuple(idx) + (slice(None),)

    def gcols(p, core):
        return pl.ds(pl.multiple_of(GSTART[p] + core * GWIDTH[p], 128), GWIDTH[p])

    def ocols(p, core):
        return pl.ds(pl.multiple_of(OSTART[p] + core * OWIDTH[p], 128), OWIDTH[p])

    def vcols(p):
        return pl.ds(VSTART[p], OWIDTH[p])

    small = [
        pltpu.make_async_copy(h, v, wsem.at[3 + i])
        for i, (h, v) in enumerate(
            ((x_hbm, x_ref), (gain_hbm, gain_ref), (ids_hbm, ids_ref), (rw_hbm, rw_ref))
        )
    ]
    for load in small:
        load.start()
    loads = [
        pltpu.make_async_copy(h, v, wsem.at[i])
        for i, (h, v) in enumerate(((wg_hbm, WG), (wu_hbm, WU), (wd_hbm, WD)))
    ]
    for load in loads:
        load.start()

    barrier = pltpu.get_barrier_semaphore()
    def across(dev):
        return (dev[0] + 1 - 2 * c, dev[1])

    partners = [sibling]
    for a in range(3):
        for s in STEPS:
            partners += [device(a, s), across(device(a, s))]
    for dev in partners:
        pl.semaphore_signal(barrier, inc=1, device_id=dev, device_id_type=MESH)

    for load in small:
        load.wait()

    lane = lax.broadcasted_iota(jnp.int32, (8, 128), 1)
    spread = jnp.zeros((8, 128), F32)
    for k in range(8):
        spread = spread + jnp.where(ids_ref[:, k : k + 1] == lane, rw_ref[:, k : k + 1], 0.0)
    high = spread.astype(BF)
    low = (spread - high.astype(F32)).astype(BF)
    stream = x_ref[...].astype(F32)
    inverse = lax.rsqrt(jnp.sum(stream * stream, axis=-1, keepdims=True) * (1.0 / 4096) + 1e-06)
    normed = (stream * inverse * gain_ref[...].astype(F32).reshape(1, 4096)).astype(BF)
    XB[:, 0:HI] = normed[:, 0:HI]
    XB[:, HI : HI + 128] = high
    XB[:, HI + 128 : LO] = normed[:, HI:4096]
    XB[:, LO:XW] = low

    er = lax.broadcasted_iota(jnp.int32, (256, 768), 0) % 128
    ec = lax.broadcasted_iota(jnp.int32, (256, 768), 1)
    held = er - 4 * expert
    E[...] = jnp.where((ec >= held * 192) & (ec < held * 192 + 192), 1.0, 0.0).astype(BF)

    @pl.loop(0, 16)
    def _(i):
        G[i // 4, i % 4] = jnp.zeros((4, 16, 768), F32)
        U[i // 4, i % 4] = jnp.zeros((4, 16, 768), F32)

    pl.semaphore_wait(barrier, len(partners))
    sends = []

    def start(cp):
        cp.start()
        sends.append(cp)

    def drain(count=None):
        for cp in sends[:count]:
            cp.wait_send()
        del sends[:count]

    def landed(key, ref):
        copy(key, ref, ref, sibling).wait_recv()

    def gline(p, b_step, k_step):
        return X.at[line_at(p, b_step, k_step) + (gcols(p, c),)]

    def send_line(p, s, b_step):
        start(
            copy(
                ("g3", p, s, b_step), gline(p, b_step, 0), gline(p, b_step, 0),
                device(ORDER[p][2], s),
            )
        )

    def stage1(p):
        a = ORDER[p][0]
        mine, other = gcols(p, c), gcols(p, 1 - c)
        start(copy(("g0", p), XB.at[:, other], XS.at[0, c, :, other], sibling))
        for i, s in enumerate(STEPS):
            dev = device(a, s)
            start(copy(("g1", p, s, 0), XB.at[:, mine], XS.at[i + 1, c, :, mine], dev))
            start(copy(("g1", p, s, 1), XB.at[:, other], XS.at[i + 1, c, :, other], across(dev)))

    def gblock(p, b_step, a_step):
        a, b, _ = ORDER[p]
        n = list(m)
        n[a], n[b] = coord(a, a_step), coord(b, b_step)
        return (n[0], n[1], n[2], slice(None), gcols(p, c))

    def stage2(p, i):
        b = ORDER[p][1]
        mine = gcols(p, c)
        if i == 0:
            XS[0, c, :, mine] = XB[:, mine]
            landed(("g0", p), XS.at[0, 1 - c, :, mine])
            a_step = 0
        else:
            a_step = -STEPS[i - 1]
            landed(("g1", p, STEPS[i - 1], 0), XS.at[i, c, :, mine])
            landed(("g1", p, STEPS[i - 1], 1), XS.at[i, 1 - c, :, mine])
        rows = jnp.concatenate(
            [XS[i, 0, :, mine].astype(F32), XS[i, 1, :, mine].astype(F32)], axis=0
        )
        X[gblock(p, 0, a_step)] = rows.astype(BF)
        ref = X.at[gblock(p, 0, a_step)]
        for s in STEPS:
            start(copy(("g2", p, s, i), ref, ref, device(b, s)))

    def xplane(p, q, core):
        return X.at[plane_index(ORDER[p][2], q) + (slice(None), gcols(p, core))]

    def stage3(p):
        k = ORDER[p][2]
        for i in range(4):
            for s in STEPS:
                a_step = 0 if i == 0 else -STEPS[i - 1]
                landed(("g2", p, s, i), X.at[gblock(p, -s, a_step)])
        for n in (1, 2, 3):
            send_line(p, 1, n)
            send_line(p, -1, 4 - n)
        ref = xplane(p, m[k], c)
        start(copy(("gs", p, 0), ref, ref, sibling))

    def relay(p, s, b_step):
        ref = gline(p, b_step, -s)
        landed(("g3", p, s, b_step), ref)
        start(copy(("gr", p, s, b_step), ref, ref, device(ORDER[p][2], s)))
        start(copy(("gl", p, s, b_step), ref, ref, sibling))

    def share(p, s, b_step):
        ref = gline(p, b_step, -s)
        landed(("g3", p, s, b_step), ref)
        start(copy(("gl", p, s, b_step), ref, ref, sibling))

    def share_far(p):
        for s, n in ((1, 0), (-1, 3), (1, 1), (-1, 2)):
            ref = gline(p, n, 2)
            landed(("gr", p, s, n), ref)
            start(copy(("gl", p, 2, n), ref, ref, sibling))

    def unit(p, s):
        k = ORDER[p][2]
        q = coord(k, -s)
        if s == 0:
            landed(("gs", p, 0), xplane(p, q, 1 - c))
        else:
            for n in range(4):
                landed(("gl", p, s, n), X.at[line_at(p, n, -s) + (gcols(p, 1 - c),)])
        index = plane_index(k, q)
        x0, xn = XK[p]
        w0, wn = WK[p]

        xs = X[index + (slice(None), slice(x0, x0 + xn))].reshape(256, xn)
        for w, acc in ((WG, G), (WU, U)):
            r = lax.dot_general(xs, w[:, w0 : w0 + wn], NT, preferred_element_type=F32)
            acc[index] += r.reshape(4, 4, 16, 768)

    for p in range(3):
        stage1(p)

    for i in range(4):
        for p in range(3):
            stage2(p, i)
    for p in range(3):
        send_line(p, 1, 0)
        send_line(p, -1, 0)
    early = len(sends)
    for p in range(3):
        stage3(p)
    for p in range(3):
        relay(p, 1, 0)
        share(p, -1, 0)
    loads[0].wait()
    loads[1].wait()
    drain(early)
    for p in range(3):
        unit(p, 0)
    for p in range(3):
        relay(p, -1, 3)
        relay(p, 1, 1)
    for p in range(3):
        relay(p, -1, 2)
        share(p, 1, 2)
    for p in range(3):
        share(p, 1, 3)
        share(p, -1, 1)
    for p in range(3):
        unit(p, 1)
    drain()
    for p in range(3):
        share_far(p)
    for p in range(3):
        unit(p, -1)
    for p in range(3):
        unit(p, 2)
    loads[2].wait()
    drain()

    @pl.loop(0, 4)
    def _(i):
        g = G[i].reshape(256, 768)
        u = U[i].reshape(256, 768)
        hi = X[i, :, :, :, HI : HI + 128].reshape(256, 128)
        lo = X[i, :, :, :, LO:XW].reshape(256, 128)
        w = jnp.dot(jnp.concatenate([hi, lo], axis=1), E[...], preferred_element_type=F32)
        A[i] = (g / (1.0 + jnp.exp(-g)) * u * w).astype(BF).reshape(4, 4, 16, 768)

    def down(p, s):
        k = ORDER[p][2]
        q = coord(k, s)
        index = plane_index(k, q)
        cs = slice(OSTART[p], OSTART[p] + 2 * OWIDTH[p])
        r = jnp.dot(A[index].reshape(256, 768), WD[:, cs], preferred_element_type=F32)
        X[index + (slice(None), cs)] = r.astype(BF).reshape(4, 4, 16, 2 * OWIDTH[p])

        start(
            copy(
                ("rs", p, s),
                X.at[index + (slice(None), ocols(p, 1 - c))],
                V.at[index + (slice(None), vcols(p))],
                sibling,
            )
        )

    def row_index(axis, q, i):
        rest = [a for a in range(3) if a != axis]
        idx = [None] * 3
        idx[axis] = q
        idx[rest[0]] = i
        idx[rest[1]] = slice(None)
        return tuple(idx)

    def paired(p, s):
        k = ORDER[p][2]
        q = coord(k, s)
        landed(("rs", p, s), V.at[plane_index(k, q) + (slice(None), vcols(p))])

        @pl.loop(0, 4)
        def _(i):
            at = row_index(k, q, i)
            o = at + (slice(None), ocols(p, c))
            X[o] = (X[o].astype(F32) + V[at + (slice(None), vcols(p))].astype(F32)).astype(BF)

    def oline(p, b_step, k_step):
        return line_at(p, b_step, k_step) + (ocols(p, c),)

    def send_far(p):
        for s, n in ((1, 1), (-1, 3), (1, 2), (-1, 0)):
            start(
                copy(
                    ("ra", p, s, n), X.at[oline(p, n, 2)], RA.at[n, :, :, vcols(p)],
                    device(ORDER[p][2], s),
                )
            )

    def send_near(p, s, n):
        start(
            copy(
                ("rf", p, s, n), X.at[oline(p, n, s)],
                RF.at[0 if s == 1 else 1, n, :, :, vcols(p)], device(ORDER[p][2], s),
            )
        )

    def relay_back(p, s, n):
        landed(("ra", p, s, n), RA.at[n, :, :, vcols(p)])
        o = oline(p, n, s)
        X[o] = (X[o].astype(F32) + RA[n, :, :, vcols(p)].astype(F32)).astype(BF)
        send_near(p, s, n)

    def ring_total(p, n):
        for slot, s in ((0, 1), (1, -1)):
            landed(("rf", p, s, n), RF.at[slot, n, :, :, vcols(p)])
        return (
            X[oline(p, n, 0)].astype(F32)
            + RF[0, n, :, :, vcols(p)].astype(F32)
            + RF[1, n, :, :, vcols(p)].astype(F32)
        )

    def pass_line(p, n):
        X[oline(p, n, 0)] = ring_total(p, n).astype(BF)
        start(
            copy(
                ("r2", p, n), X.at[oline(p, n, 0)], R2.at[n - 1, :, :, vcols(p)],
                device(ORDER[p][1], n),
            )
        )

    def own_line(p):
        X[oline(p, 0, 0)] = ring_total(p, 0).astype(BF)

    def gather_lines(p):
        a = ORDER[p][0]
        for n in range(3):
            landed(("r2", p, n + 1), R2.at[n, :, :, vcols(p)])
        o = oline(p, 0, 0)
        total = X[o].astype(F32)
        for n in range(3):
            total = total + R2[n, :, :, vcols(p)].astype(F32)
        SB[:, 0, :, vcols(p)] = total[:, 0:8].astype(BF)
        SB[:, 1, :, vcols(p)] = total[:, 8:16].astype(BF)
        for n, s in enumerate(STEPS):
            dev, at = device(a, s), coord(a, s)
            for kind, core, to in ((0, c, dev), (1, 1 - c, across(dev))):
                start(
                    copy(
                        ("r3", p, s, kind), SB.at[at, core, :, vcols(p)],
                        R3.at[n + 1, kind, :, vcols(p)], to,
                    )
                )
        start(
            copy(("r4", p), SB.at[m[a], 1 - c, :, vcols(p)], R3.at[0, 1, :, vcols(p)], sibling)
        )

    def gather_blocks(p):
        landed(("r4", p), R3.at[0, 1, :, vcols(p)])
        for n, s in enumerate(STEPS):
            for kind in range(2):
                landed(("r3", p, s, kind), R3.at[n + 1, kind, :, vcols(p)])
        mine = SB[m[ORDER[p][0]], c, :, vcols(p)].astype(F32)
        other = R3[0, 1, :, vcols(p)].astype(F32)
        for n in range(1, 4):
            mine = mine + R3[n, 0, :, vcols(p)].astype(F32)
            other = other + R3[n, 1, :, vcols(p)].astype(F32)
        out_ref[:, ocols(p, c)] = mine
        out_ref[:, ocols(p, 1 - c)] = other

    for p in range(3):
        down(p, 2)
    for p in range(3):
        down(p, 1)
        paired(p, 2)
        send_far(p)
    for p in range(3):
        down(p, -1)
        paired(p, 1)
        send_near(p, 1, 3)
    for p in range(3):
        down(p, 0)
        paired(p, -1)
        send_near(p, -1, 1)
        send_near(p, -1, 2)
    for p in range(3):
        paired(p, 0)
    for p in range(3):
        relay_back(p, 1, 1)
        relay_back(p, -1, 3)
    for p in range(3):
        relay_back(p, 1, 2)
        relay_back(p, -1, 0)
        send_near(p, 1, 0)
    for n in (1, 2, 3):
        for p in range(3):
            pass_line(p, n)
    for p in range(3):
        own_line(p)
    drain()
    for p in range(3):
        gather_lines(p)
    for p in range(3):
        gather_blocks(p)
    drain()


def local(stream_in, norm_gain, expert_ids, route_weights, w_gate, w_up, w_down):
    hidden, features = w_gate.shape[0] * w_gate.shape[1], w_gate.shape[2]
    vmem = pl.BlockSpec(memory_space=pltpu.VMEM)
    hbm = pl.BlockSpec(memory_space=pl.ANY)
    return pl.pallas_call(
        functools.partial(body, table={}),
        name="moe",
        out_shape=jax.ShapeDtypeStruct((8, 4096), F32),
        in_specs=[hbm] * 7,
        out_specs=vmem,
        scratch_shapes=[
            pltpu.VMEM((8, 4096), BF),
            pltpu.VMEM((4096,), BF),
            pltpu.VMEM((8, 8), jnp.int32),
            pltpu.VMEM((8, 8), F32),
            pltpu.VMEM((4, 4, 4, 16, XW), BF),
            pltpu.VMEM((8, XW), BF),
            pltpu.VMEM((4, 2, 8, XW), BF),
            pltpu.VMEM((768, 4096), BF),
            pltpu.VMEM((768, 4096), BF),
            pltpu.VMEM((768, 4096), BF),
            pltpu.VMEM((4, 4, 4, 16, 768), F32),
            pltpu.VMEM((4, 4, 4, 16, 768), F32),
            pltpu.VMEM((4, 4, 4, 16, 768), BF),
            pltpu.VMEM((4, 4, 4, 16, 2048), BF),
            pltpu.VMEM((4, 4, 16, 2048), BF),
            pltpu.VMEM((2, 4, 4, 16, 2048), BF),
            pltpu.VMEM((3, 4, 16, 2048), BF),
            pltpu.VMEM((4, 2, 8, 2048), BF),
            pltpu.VMEM((4, 2, 8, 2048), BF),
            pltpu.VMEM((256, 768), BF),
            pltpu.SemaphoreType.DMA((224,)),
            pltpu.SemaphoreType.DMA((224,)),
            pltpu.SemaphoreType.DMA((7,)),
        ],
        compiler_params=pltpu.CompilerParams(
            collective_id=0, has_side_effects=True, vmem_limit_bytes=60 << 20
        ),
    )(
        stream_in,
        norm_gain,
        expert_ids,
        route_weights,
        w_gate.reshape(hidden, features),
        w_up.reshape(hidden, features),
        w_down.reshape(hidden, features),
    )


def solution(mesh):
    return jax.shard_map(
        local,
        mesh=mesh,
        in_specs=(
            P(("attn", "expert"), None),
            P(),
            P(("attn", "expert"), None),
            P(("attn", "expert"), None),
            P("expert", "attn", None),
            P("expert", "attn", None),
            P("expert", "attn", None),
        ),
        out_specs=P(("attn", "expert"), None),
        check_vma=False,
    )
```
